256 devices in a mesh: row: 16 (over x, y_hi, core), col: 16 (over y_lo, z).
Axes of the slice: x: 4, y: 4 (y_hi: 2, y_lo: 2; y = y_hi * 2 + y_lo), z: 8, core: 2. Of those that a mesh axis runs over, the one named last changes fastest.
Arguments:
- query_in: bfloat16 [4096, 8192], P('row', 'col'), may hold values from -6 to 6
- key_in: bfloat16 [4096, 8192], P('row', 'col'), may hold values from -6 to 6
- value_in: bfloat16 [4096, 8192], P('row', 'col'), may hold values from -6 to 6
- filters: float32 [512, 128], P('col'), may hold values from -0.5 to 0.5
- out_weight: bfloat16 [8192, 8192], P('row', 'col'), may hold values from -0.0625 to 0.0625
- out_grad: bfloat16 [4096, 8192], P('row', 'col'), may hold values from -6 to 6
Outputs:
- mixed: bfloat16 [4096, 8192], P('row', 'col')
- query_grad: bfloat16 [4096, 8192], P('row', 'col')
- key_grad: bfloat16 [4096, 8192], P('row', 'col')
- value_grad: bfloat16 [4096, 8192], P('row', 'col')
- weight_grad: bfloat16 [8192, 8192], P('row', 'col')
- filter_grad: float32 [512, 128], P('col')
The draws below stay inside these ranges and needn't reach their ends.
All inputs are finite; a program needn't handle non-finite values.
Results may differ from the reference program's by a relative error of at most 0.018.
Values may be sent and summed in bfloat16 or wider, within the bound.
A program may use at most 128 MiB of HBM per device.

```python
import math
import jax
import jax.numpy as jnp
from jax import lax

D = 8192
FILT = 128
GROUP = 16
TOK_DEV = 256
TOKENS = 4096
G = 512
N_ROW = 16
N_COL = 16


def level_of(stream_key, shape, cuts, low, largest):
    def one(dim, shards_of):
        draws = jax.random.uniform(jax.random.fold_in(jax.random.fold_in(stream_key, 6), dim), (shards_of,), jnp.float32, low / len(cuts), largest / len(cuts))
        return jnp.repeat(jnp.exp(draws), shape[dim] // shards_of).reshape((-1,) + (1,) * (len(shape) - dim - 1))

    gain = one(*cuts[0])
    for cut in cuts[1:]:
        gain = gain * one(*cut)
    return gain


def bell_draw(key, dims, spread, bound, pieces=(), kind=jnp.bfloat16):
    gain = level_of(key, dims, pieces, -0.22, 0.18) if pieces else 1.0
    drawn = jax.random.normal(key, dims, jnp.float32) * spread * gain
    return jnp.minimum(jnp.maximum(drawn, -bound), bound).astype(kind)


def setup_inputs(seed: int = 0) -> dict:
    keys = jax.random.split(jax.random.key(seed), 7)
    return {
        "query_in": bell_draw(keys[0], (TOKENS, D), 1.0, 6.0, ((0, 16), (1, 16))),
        "key_in": bell_draw(keys[1], (TOKENS, D), 1.0, 6.0, ((0, 16), (1, 16))),
        "value_in": bell_draw(keys[2], (TOKENS, D), 1.0, 6.0, ((0, 16), (1, 16))),
        "filters": bell_draw(keys[3], (G, FILT), FILT ** -0.5, 0.5, ((0, 16),), jnp.float32),
        "out_weight": bell_draw(keys[4], (D, D), D ** -0.5, 0.0625, ((0, 16), (1, 16))),
        "out_grad": bell_draw(keys[5], (TOKENS, D), 1.0, 6.0, ((0, 16), (1, 16))),
    }


def reference(query_in, key_in, value_in, filters, out_weight, out_grad):
    f32 = jnp.float32
    bf16 = jnp.bfloat16
    query32 = query_in.astype(f32)
    key32 = key_in.astype(f32)
    value32 = value_in.astype(f32)
    product = key32 * value32
    taps = jnp.repeat(filters.astype(f32), GROUP, axis=0)
    ahead = jnp.concatenate([jnp.zeros((FILT, D), f32), product], 0)

    def conv_step(m, acc):
        part = lax.dynamic_slice_in_dim(ahead, FILT - m, TOKENS, 0)
        return acc + part * lax.dynamic_index_in_dim(taps, m, 1, False)
    conv = lax.fori_loop(0, FILT, conv_step, jnp.zeros((TOKENS, D), f32))
    gated = (query32 * conv).astype(bf16)
    mixed = jnp.dot(gated, out_weight, preferred_element_type=f32).astype(bf16)
    width = D // N_COL

    def grad_step(acc, index):
        start = (index * width).astype(jnp.int32)
        cols = lax.dynamic_slice_in_dim(out_grad, start, width, 1)
        rows = lax.dynamic_slice_in_dim(out_weight, start, width, 1)
        term = lax.dot_general(cols, rows, (((1,), (1,)), ((), ())), preferred_element_type=f32)
        term = lax.optimization_barrier(term.astype(bf16)).astype(f32)
        return (acc + term, None)
    grad_gated, _ = lax.scan(grad_step, jnp.zeros((TOKENS, D), f32), jnp.arange(N_COL, dtype=jnp.int32))
    query_grad = (grad_gated * conv).astype(bf16)
    grad_conv = grad_gated * query32
    behind = jnp.concatenate([grad_conv, jnp.zeros((FILT, D), f32)], 0)

    def back_step(m, acc):
        part = lax.dynamic_slice_in_dim(behind, m, TOKENS, 0)
        return acc + part * lax.dynamic_index_in_dim(taps, m, 1, False)
    grad_product = lax.fori_loop(0, FILT, back_step, jnp.zeros((TOKENS, D), f32))
    key_grad = (grad_product * value32).astype(bf16)
    value_grad = (grad_product * key32).astype(bf16)

    def filter_tap(m):
        part = lax.dynamic_slice_in_dim(ahead, FILT - m, TOKENS, 0)
        return lax.optimization_barrier(jnp.sum((grad_conv * part).reshape(TOKENS, D // GROUP, GROUP), axis=(0, 2)))
    per_tap = lax.map(filter_tap, jnp.arange(FILT, dtype=jnp.int32))
    filter_grad = per_tap.T * (1.0 / math.sqrt(TOKENS * GROUP))

    def weight_step(acc, index):
        start = (index * TOK_DEV).astype(jnp.int32)
        rows_a = lax.dynamic_slice_in_dim(gated, start, TOK_DEV, 0)
        rows_b = lax.dynamic_slice_in_dim(out_grad, start, TOK_DEV, 0)
        term = lax.dot_general(rows_a, rows_b, (((0,), (0,)), ((), ())), preferred_element_type=f32)
        term = lax.optimization_barrier(term.astype(bf16)).astype(f32)
        return (acc + term, None)
    weight_sum, _ = lax.scan(weight_step, jnp.zeros((D, D), f32), jnp.arange(N_ROW, dtype=jnp.int32))
    weight_grad = (weight_sum * (1.0 / math.sqrt(TOKENS))).astype(bf16)
    return (mixed, query_grad, key_grad, value_grad, weight_grad, filter_grad)
```

```python
import math

import jax
import jax.numpy as jnp
from jax import lax
from jax.experimental import pallas as pl
from jax.experimental.pallas import tpu as pltpu
from jax.sharding import PartitionSpec as P

F32 = jnp.float32
BF16 = jnp.bfloat16
MESH = pl.DeviceIdType.MESH
NT = (((1,), (1,)), ((), ()))
TN = (((0,), (0,)), ((), ()))
NN = (((1,), (0,)), ((), ()))


def dot(a, b, dims=NN):
    return lax.dot_general(a, b, dims, preferred_element_type=F32)


def split(x):
    high = x.astype(BF16)
    return high, (x - high.astype(F32)).astype(BF16)


def kernel(
    q_ref, k_ref, v_ref, f_ref, fr_ref, w_ref, og_ref,
    mixed_ref, qg_ref, kg_ref, vg_ref, wg_ref, fg_ref,
    k_rim, v_rim, g_send, g_rim,
    t_hi, t_lo, a_hi, a_lo, x_hi, x_lo, conv, gc,
    wp, gp, pb, rp, pair, wb, sb, xfar, xnear, yb,
    taps, taps_in, acc, ss, rs, ls,
):
    tok, wid = q_ref.shape
    span = f_ref.shape[1]
    groups = f_ref.shape[0]
    group = wid // groups
    lanes = 128
    tiles = wid // lanes
    per = lanes // group
    half = tok // 2
    whalf = wid // 2

    r = lax.axis_index("row")
    c = lax.axis_index("col")
    x, yh, core = r // 4, lax.rem(r // 2, 2), lax.rem(r, 2)
    yl, z = c // 8, lax.rem(c, 8)

    def rowid(dx, flip_y, flip_core):
        yy = 1 - yh if flip_y else yh
        cc = 1 - core if flip_core else core
        return lax.rem(x + dx + 4, 4) * 4 + yy * 2 + cc

    def colid(dz, flip_y):
        yy = 1 - yl if flip_y else yl
        return yy * 8 + lax.rem(z + dz + 8, 8)

    sib = (rowid(0, 0, 1), c)
    ytwo = (rowid(0, 1, 0), c)
    xdev = {1: (rowid(1, 0, 0), c), -1: (rowid(-1, 0, 0), c)}
    zdev = {1: (r, colid(1, 0)), -1: (r, colid(-1, 0))}
    ypair = (r, colid(0, 1))
    after = (lax.rem(r + 1, 16), c)
    before = (lax.rem(r + 15, 16), c)

    barrier = pltpu.get_barrier_semaphore()
    peers = [sib, ytwo, xdev[1], xdev[-1], zdev[1], zdev[-1], ypair, after, before]
    for peer in peers:
        pl.semaphore_signal(barrier, inc=1, device_id=peer, device_id_type=MESH)
    pl.semaphore_wait(barrier, len(peers))

    names = {}
    started = []

    def slot(name):
        return names.setdefault(name, len(names))

    def desc(src, dst, name, dev):
        n = name if not isinstance(name, str) else slot(name)
        return pltpu.make_async_remote_copy(
            src_ref=src, dst_ref=dst, send_sem=ss.at[n], recv_sem=rs.at[n],
            device_id=dev, device_id_type=MESH,
        )

    def send(src, dst, name, dev):
        copy = desc(src, dst, name, dev)
        copy.start()
        started.append(copy)

    def recv(dst, name, dev):
        desc(dst, dst, name, dev).wait_recv()

    def add_into(dst, src):
        step = 64

        def body(i, carry):
            rows = pl.ds(pl.multiple_of(i * step, step), step)
            dst[rows, :] = (dst[rows, :].astype(F32) + src[rows, :].astype(F32)).astype(BF16)
            return carry

        lax.fori_loop(0, dst.shape[0] // step, body, 0)

    send(k_ref.at[pl.ds(tok - span, span)], k_rim, "hk", after)
    send(v_ref.at[pl.ds(tok - span, span)], v_rim, "hv", after)
    send(w_ref, wp.at[r], "w_y", ytwo)
    for s in (1, -1):
        send(w_ref, wp.at[r], f"w_x{s}", xdev[s])
    send(w_ref, wp.at[r], "w_s00", sib)
    own = pltpu.make_async_copy(w_ref, wp.at[r], ls.at[0])
    own.start()

    def shear(row, shift):
        wide = jnp.concatenate([row, jnp.zeros((1, span), F32)], axis=1)
        wide = jnp.broadcast_to(wide, (span, 2 * span))
        return pltpu.roll(wide, shift, 1, stride=1, stride_axis=0)

    def build(source, high_ref, low_ref, shift):
        def body(g, carry):
            rows = pl.ds(pl.multiple_of(g * span, span), span)
            high, low = split(shear(source[pl.ds(g, 1), :], shift))
            high_ref[rows, :] = high
            low_ref[rows, :] = low
            return carry

        lax.fori_loop(0, groups, body, 0)

    lane_group = lax.broadcasted_iota(jnp.int32, (span, 2 * lanes), 1)
    lane_group = lax.rem(lane_group, lanes) // group

    def pick(full):
        out = full[0:span]
        for g in range(1, per):
            out = jnp.where(lane_group == g, full[g * span:(g + 1) * span], out)
        return out

    def two(ref, cols):
        return jnp.concatenate(
            [ref[pl.ds(0, 2 * span), cols], ref[pl.ds(span, 2 * span), cols]], axis=1
        )

    def filtered(high_ref, low_ref, j, xh, xl):
        rows = pl.ds(pl.multiple_of(j * per * span, per * span), per * span)
        mh = high_ref[rows, :]
        full = dot(mh, xh) + dot(mh, xl) + dot(low_ref[rows, :], xh)
        return pick(full)

    build(fr_ref, t_hi, t_lo, 1)
    high, low = split(k_ref[...].astype(F32) * v_ref[...].astype(F32))
    x_hi[pl.ds(span, tok), :] = high
    x_lo[pl.ds(span, tok), :] = low
    recv(k_rim, "hk", before)
    recv(v_rim, "hv", before)
    rim = k_rim[...].astype(F32) * v_rim[...].astype(F32)
    high, low = split(jnp.where(r > 0, rim, 0.0))
    x_hi[pl.ds(0, span), :] = high
    x_lo[pl.ds(0, span), :] = low

    def forward(j, carry):
        cols = pl.ds(pl.multiple_of(j * lanes, lanes), lanes)
        out = filtered(t_hi, t_lo, j, two(x_hi, cols), two(x_lo, cols))
        for b in range(2):
            rows = pl.ds(b * span, span)
            part = out[:, b * lanes:(b + 1) * lanes]
            conv[rows, cols] = part
            gp[c, rows, cols] = (q_ref[rows, cols].astype(F32) * part).astype(BF16)
        return carry

    lax.fori_loop(0, tiles, forward, 0)

    send(gp.at[c], gp.at[c], "g_y", ypair)
    for s in (1, -1):
        send(gp.at[c], gp.at[c], f"g_{s}_0_1", zdev[s])

    def w_half(s):
        return pl.ds(0 if s == 1 else whalf, whalf)

    def g_half(s):
        return pl.ds(0 if s == 1 else half, half)

    def w_near(flip):
        for s in (1, -1):
            blk = rowid(-s, flip, 0)
            name = f"w_x{s}" if not flip else f"w_yx{s}"
            recv(wp.at[blk], name, xdev[-s])
            rows = w_half(s)
            send(wp.at[blk, rows], wp.at[blk, rows], f"w_far{s}_{flip}", xdev[s])
            send(wp.at[blk], wp.at[blk], f"w_s{s}{flip}", sib)

    def g_step(flip, dist):
        for s in (1, -1):
            blk = colid(-s * dist, flip)
            recv(gp.at[blk], f"g_{s}_{flip}_{dist}", zdev[-s])
            if dist < 3:
                send(gp.at[blk], gp.at[blk], f"g_{s}_{flip}_{dist + 1}", zdev[s])
            else:
                rows = g_half(s)
                send(gp.at[blk, rows], gp.at[blk, rows], f"g_{s}_{flip}_4", zdev[s])

    w_near(0)
    blk = colid(0, 1)
    recv(gp.at[blk], "g_y", ypair)
    for s in (1, -1):
        send(gp.at[blk], gp.at[blk], f"g_{s}_1_1", zdev[s])
    g_step(0, 1)
    build(f_ref, a_hi, a_lo, 0)
    blk = rowid(0, 1, 0)
    recv(wp.at[blk], "w_y", ytwo)
    for s in (1, -1):
        send(wp.at[blk], wp.at[blk], f"w_yx{s}", xdev[s])
    send(wp.at[blk], wp.at[blk], "w_s01", sib)
    g_step(1, 1)
    g_step(0, 2)
    w_near(1)
    g_step(1, 2)
    g_step(0, 3)
    for flip in (0, 1):
        blk = rowid(2, flip, 0)
        for s in (1, -1):
            rows = w_half(s)
            recv(wp.at[blk, rows], f"w_far{s}_{flip}", xdev[-s])
        send(wp.at[blk], wp.at[blk], f"w_s2{flip}", sib)
    g_step(1, 3)
    own.wait()
    for flip in (0, 1):
        recv(wp.at[rowid(0, flip, 1)], f"w_s0{flip}", sib)
        for s in (1, -1):
            recv(wp.at[rowid(-s, flip, 1)], f"w_s{s}{flip}", sib)
        recv(wp.at[rowid(2, flip, 1)], f"w_s2{flip}", sib)

    def partial(i, carry):
        pb[i] = dot(og_ref[...], wp[i], NT).astype(BF16)
        return carry

    lax.fori_loop(0, 16, partial, 0)

    def p_send(flip, dist):
        for n, s in enumerate((1, -1)):
            dest = colid(s * dist, flip)
            if dist == 4:
                rows = g_half(s)
                send(pb.at[dest, rows], rp.at[n, flip, 3, rows], f"p_{s}_{flip}_4", zdev[s])
                continue
            if dist == 3:
                rows = g_half(s)
                recv(rp.at[n, flip, 3, rows], f"p_{s}_{flip}_4", zdev[-s])
                add_into(pb.at[dest, rows], rp.at[n, flip, 3, rows])
            else:
                recv(rp.at[n, flip, dist], f"p_{s}_{flip}_{dist + 1}", zdev[-s])
                add_into(pb.at[dest], rp.at[n, flip, dist])
            send(pb.at[dest], rp.at[n, flip, dist - 1], f"p_{s}_{flip}_{dist}", zdev[s])

    p_send(1, 4)
    p_send(0, 4)
    for flip in (0, 1):
        blk = colid(4, flip)
        for s in (1, -1):
            rows = g_half(s)
            recv(gp.at[blk, rows], f"g_{s}_{flip}_4", zdev[-s])

    order = [(2, 1), (2, 0), (1, 1), (-1, 1), (1, 0), (-1, 0), (0, 1), (0, 0)]
    sib_base = slot("s_0")
    for i in range(1, 8):
        slot(f"s_{i}")

    def order_row(i, cc):
        dx = jnp.where(i < 2, 2, jnp.where(i >= 6, 0, jnp.where(lax.rem(i, 2) == 0, 1, 3)))
        flip = jnp.where(i < 2, 1 - i, jnp.where(i >= 6, 7 - i, jnp.where(i < 4, 1, 0)))
        yy = lax.rem(yh + flip, 2)
        return lax.rem(x + dx, 4) * 4 + yy * 2 + cc

    def for_sib(i, carry):
        dest = order_row(i, 1 - core)
        wb[dest] = dot(gp[dest], og_ref[...], TN).astype(BF16)
        desc(wb.at[dest], sb.at[i], sib_base + i, sib).start()
        return carry

    def for_own(i, carry):
        dest = order_row(i, core)
        part = dot(gp[dest], og_ref[...], TN)
        desc(sb.at[i], sb.at[i], sib_base + i, sib).wait_recv()
        wb[dest] = (part + sb[i].astype(F32)).astype(BF16)
        return carry

    def wx_far(flip):
        for n, s in enumerate((1, -1)):
            dest = rowid(2, flip, 0)
            rows = w_half(s)
            send(wb.at[dest, rows], xfar.at[n, flip], f"x_far{s}_{flip}", xdev[s])

    def wx_near(flip):
        for n, s in enumerate((1, -1)):
            dest = rowid(s, flip, 0)
            rows = w_half(s)
            recv(xfar.at[n, flip], f"x_far{s}_{flip}", xdev[-s])
            add_into(wb.at[dest, rows], xfar.at[n, flip])
            send(wb.at[dest], xnear.at[n, flip], f"x_near{s}_{flip}", xdev[s])

    lax.fori_loop(0, 8, for_sib, 0)
    p_send(1, 3)
    p_send(0, 3)
    lax.fori_loop(0, 2, for_own, 0)
    wx_far(1)
    wx_far(0)
    lax.fori_loop(2, 8, for_own, 0)
    p_send(1, 2)
    p_send(0, 2)
    wx_near(1)
    wx_near(0)

    acc[...] = jnp.zeros_like(acc)

    def mix(i, carry):
        acc[...] += dot(gp[i], wp[i])
        return carry

    lax.fori_loop(0, 8, mix, 0)
    p_send(1, 1)
    p_send(0, 1)
    lax.fori_loop(8, 16, mix, 0)
    mixed_ref[...] = acc[...].astype(BF16)

    def w_total(flip):
        dest = rowid(0, flip, 0)
        for n, s in enumerate((1, -1)):
            recv(xnear.at[n, flip], f"x_near{s}_{flip}", xdev[-s])
            add_into(wb.at[dest], xnear.at[n, flip])

    w_total(1)
    send(wb.at[rowid(0, 1, 0)], yb, "x_y", ytwo)

    blk = colid(0, 1)
    for n, s in enumerate((1, -1)):
        recv(rp.at[n, 1, 0], f"p_{s}_1_1", zdev[-s])
        add_into(pb.at[blk], rp.at[n, 1, 0])
    send(pb.at[blk], pair, "p_y", ypair)
    for n, s in enumerate((1, -1)):
        recv(rp.at[n, 0, 0], f"p_{s}_0_1", zdev[-s])
    recv(pair, "p_y", ypair)
    step = 64

    def gradients(i, carry):
        rows = pl.ds(pl.multiple_of(i * step, step), step)
        total = pb[c, rows, :].astype(F32) + rp[0, 0, 0, rows, :].astype(F32)
        total += rp[1, 0, 0, rows, :].astype(F32) + pair[rows, :].astype(F32)
        qg_ref[rows, :] = (total * conv[rows, :]).astype(BF16)
        grad = total * q_ref[rows, :].astype(F32)
        gc[rows, :] = grad
        return carry

    lax.fori_loop(0, tok // step, gradients, 0)
    g_send[...] = gc[pl.ds(0, span), :].astype(BF16)
    send(g_send, g_rim, "g_rim", before)

    def corr(j, carry):
        cols = pl.ds(pl.multiple_of(j * lanes, lanes), lanes)
        grad = jnp.concatenate([gc[pl.ds(0, span), cols], gc[pl.ds(span, span), cols]], axis=1)
        masked = jnp.concatenate(
            [jnp.where(lane_group == g, grad, 0.0) for g in range(per)], axis=0
        )
        gh, gl = split(masked)
        xh = two(x_hi, cols)
        xl = two(x_lo, cols)
        full = dot(gh, xh, NT) + dot(gh, xl, NT) + dot(gl, xh, NT)
        for g in range(per):
            block = full[g * span:(g + 1) * span]
            size = span
            while size > 8:
                size //= 2
                block = block[0:size] + pltpu.roll(block[size:2 * size], 2 * span - size, 1)
            sub = lax.broadcasted_iota(jnp.int32, (8, 2 * span), 0)
            for bit in (4, 2, 1):
                moved = pltpu.roll(block, 2 * span - bit, 1)
                block = jnp.where((sub // bit) % 2 == 1, moved, block)
            line = jnp.sum(block, axis=0, keepdims=True)
            taps[pl.ds(j * per + g, 1), :] = line
        return carry

    lax.fori_loop(0, tiles, corr, 0)

    recv(g_rim, "g_rim", after)
    own_taps = taps_in.at[0]
    own_taps[...] = taps[:, pl.ds(0, 2 * span)][:, 1:span + 1]
    odd = lax.rem(x, 2)
    hop_a = (lax.rem(x + 1 - 2 * odd + 4, 4) * 4 + yh * 2 + core, c)
    hop_b = (lax.rem(x - 1 + 2 * odd + 4, 4) * 4 + yh * 2 + core, c)
    hops = [sib, hop_a, hop_b, ytwo]

    def backward(j, carry):
        cols = pl.ds(pl.multiple_of(j * lanes, lanes), lanes)
        rimv = jnp.where(r < 15, g_rim[:, cols].astype(F32), 0.0)
        lower = gc[pl.ds(0, span), cols]
        upper = gc[pl.ds(span, span), cols]
        ext = jnp.concatenate(
            [jnp.concatenate([lower, upper], axis=0), jnp.concatenate([upper, rimv], axis=0)],
            axis=1,
        )
        xh, xl = split(ext)
        out = filtered(a_hi, a_lo, j, xh, xl)
        for b in range(2):
            rows = pl.ds(b * span, span)
            part = out[:, b * lanes:(b + 1) * lanes]
            kg_ref[rows, cols] = (part * v_ref[rows, cols].astype(F32)).astype(BF16)
            vg_ref[rows, cols] = (part * k_ref[rows, cols].astype(F32)).astype(BF16)
        return carry

    for n, hop in enumerate(hops):
        send(taps_in.at[2 * n], taps_in.at[2 * n + 1], f"t_{n}", hop)
        lax.fori_loop(n, n + 1, backward, 0)
        recv(taps_in.at[2 * n + 1], f"t_{n}", hop)
        taps_in[2 * n + 2] = taps_in[2 * n] + taps_in[2 * n + 1]
    fg_ref[...] = taps_in[8] * (1.0 / math.sqrt(tok * 16 * group))

    w_total(0)
    recv(yb, "x_y", ytwo)
    final = wb.at[r]
    scale = 1.0 / math.sqrt(tok * 16)

    def finish(i, carry):
        rows = pl.ds(pl.multiple_of(i * step, step), step)
        wg_ref[rows, :] = (
            (final[rows, :].astype(F32) + yb[rows, :].astype(F32)) * scale
        ).astype(BF16)
        return carry

    lax.fori_loop(0, wid // step, finish, 0)

    for copy in started:
        copy.wait_send()

    def drain(i, carry):
        desc(wb.at[0], sb.at[i], sib_base + i, sib).wait_send()
        return carry

    lax.fori_loop(0, 8, drain, 0)
    assert len(names) <= ss.shape[0], len(names)


def shards(query_in, key_in, value_in, filters, out_weight, out_grad):
    tok, wid = query_in.shape
    groups, span = filters.shape
    act = jax.ShapeDtypeStruct((tok, wid), BF16)
    vmem = pl.BlockSpec(memory_space=pltpu.VMEM)
    sems = 96
    mixed, qg, kg, vg, wg, fg = pl.pallas_call(
        kernel,
        out_shape=(
            act, act, act, act,
            jax.ShapeDtypeStruct((wid, wid), BF16),
            jax.ShapeDtypeStruct((groups, span), F32),
        ),
        in_specs=[vmem] * 7,
        out_specs=[vmem] * 6,
        scratch_shapes=[
            pltpu.VMEM((span, wid), BF16),
            pltpu.VMEM((span, wid), BF16),
            pltpu.VMEM((span, wid), BF16),
            pltpu.VMEM((span, wid), BF16),
            pltpu.VMEM((groups * span, 2 * span), BF16),
            pltpu.VMEM((groups * span, 2 * span), BF16),
            pltpu.VMEM((groups * span, 2 * span), BF16),
            pltpu.VMEM((groups * span, 2 * span), BF16),
            pltpu.VMEM((span + tok, wid), BF16),
            pltpu.VMEM((span + tok, wid), BF16),
            pltpu.VMEM((tok, wid), F32),
            pltpu.VMEM((tok, wid), F32),
            pltpu.VMEM((16, wid, wid), BF16),
            pltpu.VMEM((16, tok, wid), BF16),
            pltpu.VMEM((16, tok, wid), BF16),
            pltpu.VMEM((2, 2, 4, tok, wid), BF16),
            pltpu.VMEM((tok, wid), BF16),
            pltpu.VMEM((16, wid, wid), BF16),
            pltpu.VMEM((8, wid, wid), BF16),
            pltpu.VMEM((2, 2, wid // 2, wid), BF16),
            pltpu.VMEM((2, 2, wid, wid), BF16),
            pltpu.VMEM((wid, wid), BF16),
            pltpu.VMEM((groups, 2 * span), F32),
            pltpu.VMEM((9, groups, span), F32),
            pltpu.VMEM((tok, wid), F32),
            pltpu.SemaphoreType.DMA((sems,)),
            pltpu.SemaphoreType.DMA((sems,)),
            pltpu.SemaphoreType.DMA((1,)),
        ],
        compiler_params=pltpu.CompilerParams(
            collective_id=0, has_side_effects=True, vmem_limit_bytes=67_000_000
        ),
    )(query_in, key_in, value_in, filters, filters[:, ::-1], out_weight, out_grad)
    return mixed, qg, kg, vg, wg, fg[:, ::-1]


def solution(mesh):
    placed = (
        P("row", "col"),
        P("row", "col"),
        P("row", "col"),
        P("col", None),
        P("row", "col"),
        P("row", "col"),
    )
    return jax.shard_map(
        shards,
        mesh=mesh,
        in_specs=placed,
        out_specs=(
            P("row", "col"),
            P("row", "col"),
            P("row", "col"),
            P("row", "col"),
            P("row", "col"),
            P("col", None),
        ),
        check_vma=False,
    )
```

```python
import math

import jax
import jax.numpy as jnp
from jax import lax
from jax.experimental import pallas as pl
from jax.experimental.pallas import tpu as pltpu
from jax.sharding import PartitionSpec as P

F32 = jnp.float32
BF16 = jnp.bfloat16
MESH = pl.DeviceIdType.MESH
NT = (((1,), (1,)), ((), ()))
TN = (((0,), (0,)), ((), ()))
NN = (((1,), (0,)), ((), ()))


def dot(a, b, dims=NN):
    return lax.dot_general(a, b, dims, preferred_element_type=F32)


def split(x):
    high = x.astype(BF16)
    return high, (x - high.astype(F32)).astype(BF16)


def kernel(
    q_ref, k_ref, v_ref, f_ref, w_ref, og_ref,
    mixed_ref, qg_ref, kg_ref, vg_ref, wg_ref, fg_ref,
    k_rim, v_rim, g_rim, back,
    t_hi, t_lo, a_hi, a_lo, x_hi, x_lo, conv, gc,
    wp, gp, pb, rp, py, pair, wb, sb, xfar, xnear, yb,
    taps, tin, acc, ss, rs, ls,
):
    tok, wid = q_ref.shape
    span = f_ref.shape[1]
    groups = f_ref.shape[0]
    group = wid // groups
    lanes = 128
    tiles = wid // lanes
    per = lanes // group
    half = tok // 2
    whalf = wid // 2

    r = lax.axis_index("row")
    c = lax.axis_index("col")
    x, yh, core = r // 4, lax.rem(r // 2, 2), lax.rem(r, 2)
    yl, z = c // 8, lax.rem(c, 8)

    def rowid(dx, flip_y, flip_core):
        yy = 1 - yh if flip_y else yh
        cc = 1 - core if flip_core else core
        return lax.rem(x + dx + 4, 4) * 4 + yy * 2 + cc

    def colid(dz, flip_y):
        yy = 1 - yl if flip_y else yl
        return yy * 8 + lax.rem(z + dz + 8, 8)

    sib = (rowid(0, 0, 1), c)
    ytwo = (rowid(0, 1, 0), c)
    ysib = (rowid(0, 1, 1), c)
    xdev = {d: (rowid(d, 0, 0), c) for d in (1, -1, 2)}
    zdev = {1: (r, colid(1, 0)), -1: (r, colid(-1, 0))}
    ypair = (r, colid(0, 1))
    after = (lax.rem(r + 1, 16), c)
    before = (lax.rem(r + 15, 16), c)

    barrier = pltpu.get_barrier_semaphore()
    peers = [sib, ytwo, ysib, xdev[1], xdev[-1], xdev[2]]
    peers += [zdev[1], zdev[-1], ypair, after, before]
    for peer in peers:
        pl.semaphore_signal(barrier, inc=1, device_id=peer, device_id_type=MESH)
    pl.semaphore_wait(barrier, len(peers))

    names = {}
    started = []

    def slot(name):
        return names.setdefault(name, len(names))

    def desc(src, dst, name, dev):
        n = name if not isinstance(name, str) else slot(name)
        return pltpu.make_async_remote_copy(
            src_ref=src, dst_ref=dst, send_sem=ss.at[n], recv_sem=rs.at[n],
            device_id=dev, device_id_type=MESH,
        )

    def send(src, dst, name, dev):
        copy = desc(src, dst, name, dev)
        copy.start()
        started.append(copy)

    def recv(dst, name, dev):
        desc(dst, dst, name, dev).wait_recv()

    def add_into(dst, src):
        step = 64

        def body(i, carry):
            rows = pl.ds(pl.multiple_of(i * step, step), step)
            dst[rows, :] = (dst[rows, :].astype(F32) + src[rows, :].astype(F32)).astype(BF16)
            return carry

        lax.fori_loop(0, dst.shape[0] // step, body, 0)

    send(k_ref.at[pl.ds(tok - span, span)], k_rim, "hk", after)
    send(v_ref.at[pl.ds(tok - span, span)], v_rim, "hv", after)

    def far_half(s):
        return 0 if s == 1 else 1

    def wh(blk, h):
        return wp.at[blk, pl.ds(h * whalf, whalf)]

    for h in (0, 1):
        part = w_ref.at[pl.ds(h * whalf, whalf)]
        send(part, wh(r, h), f"w_y_{h}", ytwo)
    for k in (0, 1):
        for s in (1, -1):
            h = far_half(s) if k == 0 else 1 - far_half(s)
            part = w_ref.at[pl.ds(h * whalf, whalf)]
            send(part, wh(r, h), f"w_x{s}0_{h}", xdev[s])
    send(w_ref, wp.at[r], "w_s00", sib)
    own = pltpu.make_async_copy(w_ref, wp.at[r], ls.at[0])
    own.start()

    flip_taps = (
        lax.broadcasted_iota(jnp.int32, (span, span), 0)
        + lax.broadcasted_iota(jnp.int32, (span, span), 1)
    ) == span - 1
    flip_taps = jnp.where(flip_taps, 1.0, 0.0).astype(BF16)

    def reversed_taps(value):
        high, low = split(value)
        rest = (value - high.astype(F32) - low.astype(F32)).astype(BF16)
        return dot(high, flip_taps) + dot(low, flip_taps) + dot(rest, flip_taps)

    def shear(row, shift):
        wide = jnp.concatenate([row, jnp.zeros((1, span), F32)], axis=1)
        wide = jnp.broadcast_to(wide, (span, 2 * span))
        return pltpu.roll(wide, shift, 1, stride=1, stride_axis=0)

    def build(source, high_ref, low_ref, shift):
        def body(g, carry):
            rows = pl.ds(pl.multiple_of(g * span, span), span)
            high, low = split(shear(source[pl.ds(g, 1), :], shift))
            high_ref[rows, :] = high
            low_ref[rows, :] = low
            return carry

        lax.fori_loop(0, groups, body, 0)

    lane_group = lax.broadcasted_iota(jnp.int32, (span, 2 * lanes), 1)
    lane_group = lax.rem(lane_group, lanes) // group

    def pick(full):
        out = full[0:span]
        for g in range(1, per):
            out = jnp.where(lane_group == g, full[g * span:(g + 1) * span], out)
        return out

    def two(ref, cols):
        return jnp.concatenate(
            [ref[pl.ds(0, 2 * span), cols], ref[pl.ds(span, 2 * span), cols]], axis=1
        )

    back[...] = reversed_taps(f_ref[...])
    build(back, t_hi, t_lo, 1)
    high, low = split(k_ref[...].astype(F32) * v_ref[...].astype(F32))
    x_hi[pl.ds(span, tok), :] = high
    x_lo[pl.ds(span, tok), :] = low
    recv(k_rim, "hk", before)
    recv(v_rim, "hv", before)
    rim = k_rim[...].astype(F32) * v_rim[...].astype(F32)
    high, low = split(jnp.where(r > 0, rim, 0.0))
    x_hi[pl.ds(0, span), :] = high
    x_lo[pl.ds(0, span), :] = low

    def forward(j, carry):
        cols = pl.ds(pl.multiple_of(j * lanes, lanes), lanes)
        taps_rows = pl.ds(pl.multiple_of(j * per * span, per * span), per * span)
        mh = t_hi[taps_rows, :]
        xh = two(x_hi, cols)
        out = pick(dot(mh, xh) + dot(mh, two(x_lo, cols)) + dot(t_lo[taps_rows, :], xh))
        for b in range(2):
            rows = pl.ds(b * span, span)
            part = out[:, b * lanes:(b + 1) * lanes]
            conv[rows, cols] = part
            gp[c, rows, cols] = (q_ref[rows, cols].astype(F32) * part).astype(BF16)
        return carry

    every = pl.ds(0, tok)

    def gh(blk, h):
        return gp.at[blk, every, pl.ds(h * whalf, whalf)]

    for h in (0, 1):
        lax.fori_loop(h * tiles // 2, (h + 1) * tiles // 2, forward, 0)
        send(gh(c, h), gh(c, h), f"gy_0{h}", ypair)
        for s in (1, -1):
            send(gh(c, h), gh(c, h), f"g_{s}_0_1_{h}", zdev[s])

    def g_step(flip, dist):
        for h in (0, 1):
            for s in (1, -1):
                blk = colid(-s * dist, flip)
                if dist == 4:
                    if h == far_half(s):
                        recv(gh(blk, h), f"g_{s}_{flip}_4_{h}", zdev[-s])
                    continue
                recv(gh(blk, h), f"g_{s}_{flip}_{dist}_{h}", zdev[-s])
                onward = dist < 2 if flip else dist < 3 or h == far_half(s)
                if onward:
                    send(gh(blk, h), gh(blk, h), f"g_{s}_{flip}_{dist + 1}_{h}", zdev[s])
        if not flip and dist > 2:
            for d in (-3, 3) if dist == 3 else (4,):
                blk = colid(d, 0)
                send(gp.at[blk], gp.at[blk], f"gy_{d}", ypair)

    def w_far(flip):
        for s in (1, -1):
            blk, h = rowid(-s, flip, 0), far_half(s)
            recv(wh(blk, h), f"w_x{s}{flip}_{h}", xdev[-s])
            send(wh(blk, h), wh(blk, h), f"w_far{s}{flip}", xdev[s])

    def w_near(flip):
        for s in (1, -1):
            blk, h = rowid(-s, flip, 0), 1 - far_half(s)
            recv(wh(blk, h), f"w_x{s}{flip}_{h}", xdev[-s])
            send(wp.at[blk], wp.at[blk], f"w_s{s}{flip}", sib)

    def w_two():
        blk = rowid(0, 1, 0)
        for h in (0, 1):
            recv(wh(blk, h), f"w_y_{h}", ytwo)
        for k in (0, 1):
            for s in (1, -1):
                h = far_half(s) if k == 0 else 1 - far_half(s)
                send(wh(blk, h), wh(blk, h), f"w_x{s}1_{h}", xdev[s])
        send(wp.at[blk], wp.at[blk], "w_s01", sib)

    def w_last(flip):
        blk = rowid(2, flip, 0)
        for s in (1, -1):
            h = far_half(s)
            recv(wh(blk, h), f"w_far{s}{flip}", xdev[-s])
            send(wh(blk, h), wh(blk, h), f"w_s2{flip}_{h}", sib)

    def g_partner():
        blk = colid(0, 1)
        for h in (0, 1):
            recv(gh(blk, h), f"gy_0{h}", ypair)
            for s in (1, -1):
                send(gh(blk, h), gh(blk, h), f"g_{s}_1_1_{h}", zdev[s])

    w_far(0)
    g_step(0, 1)
    w_two()
    w_near(0)
    g_step(0, 2)
    g_partner()
    w_last(0)
    build(f_ref, a_hi, a_lo, 0)
    w_far(1)
    g_step(0, 3)
    g_step(1, 1)
    w_near(1)
    g_step(0, 4)
    w_last(1)
    own.wait()
    for flip in (0, 1):
        recv(wp.at[rowid(0, flip, 1)], f"w_s0{flip}", sib)
        for d in (1, -1):
            recv(wp.at[rowid(-d, flip, 1)], f"w_s{d}{flip}", sib)
        for h in (0, 1):
            recv(wh(rowid(2, flip, 1), h), f"w_s2{flip}_{h}", sib)

    def partial(i, carry):
        dest = lax.rem(1 - yl + i // 8, 2) * 8 + lax.rem(z + i, 8)
        pb[dest] = dot(og_ref[...], wp[dest], NT).astype(BF16)
        return carry

    def hrows(h):
        return pl.ds(h * half, half)

    def p_pass(flip, dist):
        far = 2 if flip else 4
        for h in (0, 1):
            for n, s in enumerate((1, -1)):
                hh = 1 - h if s == 1 else h
                rows = hrows(hh)
                dest = colid(s * dist, flip)
                if dist == 4 and hh != far_half(s):
                    continue
                if dist < far and not (dist == 3 and hh != far_half(s)):
                    recv(rp.at[n, flip, dist, rows], f"p_{s}_{flip}_{dist + 1}_{hh}", zdev[-s])
                    add_into(pb.at[dest, rows], rp.at[n, flip, dist, rows])
                send(
                    pb.at[dest, rows], rp.at[n, flip, dist - 1, rows],
                    f"p_{s}_{flip}_{dist}_{hh}", zdev[s],
                )

    lax.fori_loop(2, 7, partial, 0)
    for n, d in enumerate((4, 3, -3)):
        send(pb.at[colid(d, 1)], py.at[n], f"py_{d}", ypair)
    p_pass(1, 2)
    lax.fori_loop(7, 16, partial, 0)
    lax.fori_loop(0, 2, partial, 0)
    recv(py.at[0], "py_4", ypair)
    add_into(pb.at[colid(4, 0)], py.at[0])
    p_pass(0, 4)
    g_step(1, 2)
    for n, d in ((1, 3), (2, -3)):
        recv(py.at[n], f"py_{d}", ypair)
        add_into(pb.at[colid(d, 0)], py.at[n])
    p_pass(1, 1)
    p_pass(0, 3)
    for d in (-3, 3, 4):
        recv(gp.at[colid(d, 1)], f"gy_{d}", ypair)

    sib_base = slot("s_0")
    for i in range(1, 8):
        slot(f"s_{i}")

    def order_row(i, cc):
        dx = jnp.where(i < 2, 2, jnp.where(i >= 6, 0, jnp.where(lax.rem(i, 2) == 0, 1, 3)))
        flip = jnp.where(i < 2, 1 - i, jnp.where(i >= 6, 7 - i, jnp.where(i < 4, 1, 0)))
        yy = lax.rem(yh + flip, 2)
        return lax.rem(x + dx, 4) * 4 + yy * 2 + cc

    def for_sib(i, carry):
        dest = order_row(i, 1 - core)
        wb[dest] = dot(gp[dest], og_ref[...], TN).astype(BF16)
        desc(wb.at[dest], sb.at[i], sib_base + i, sib).start()
        return carry

    def for_own(i, carry):
        dest = order_row(i, core)
        part = dot(gp[dest], og_ref[...], TN)
        desc(sb.at[i], sb.at[i], sib_base + i, sib).wait_recv()
        wb[dest] = (part + sb[i].astype(F32)).astype(BF16)
        return carry

    def w_half(s):
        return pl.ds(0 if s == 1 else whalf, whalf)

    def wx_far(flip):
        for n, s in enumerate((1, -1)):
            dest = rowid(2, flip, 0)
            rows = w_half(s)
            send(wb.at[dest, rows], xfar.at[n, flip], f"x_far{s}_{flip}", xdev[s])

    def wx_near(flip):
        for n, s in enumerate((1, -1)):
            dest = rowid(s, flip, 0)
            rows = w_half(s)
            recv(xfar.at[n, flip], f"x_far{s}_{flip}", xdev[-s])
            add_into(wb.at[dest, rows], xfar.at[n, flip])
            send(wb.at[dest], xnear.at[n, flip], f"x_near{s}_{flip}", xdev[s])

    lax.fori_loop(0, 4, for_sib, 0)
    lax.fori_loop(0, 2, for_own, 0)
    wx_far(1)
    wx_far(0)
    lax.fori_loop(4, 8, for_sib, 0)
    p_pass(0, 2)
    lax.fori_loop(2, 8, for_own, 0)
    wx_near(1)
    wx_near(0)

    blk = colid(0, 1)
    for h in (0, 1):
        rows = hrows(h)
        for n, s in enumerate((1, -1)):
            recv(rp.at[n, 1, 0, rows], f"p_{s}_1_1_{h}", zdev[-s])
            add_into(pb.at[blk, rows], rp.at[n, 1, 0, rows])
    send(pb.at[blk], pair, "py_0", ypair)
    p_pass(0, 1)

    acc[...] = jnp.zeros_like(acc)

    def mix(i, carry):
        acc[...] += dot(gp[i], wp[i])
        return carry

    lax.fori_loop(0, 16, mix, 0)
    mixed_ref[...] = acc[...].astype(BF16)

    def w_total(flip):
        dest = rowid(0, flip, 0)
        for n, s in enumerate((1, -1)):
            recv(xnear.at[n, flip], f"x_near{s}_{flip}", xdev[-s])
            add_into(wb.at[dest], xnear.at[n, flip])

    w_total(1)
    send(wb.at[rowid(0, 1, 0)], yb, "x_y", ytwo)

    recv(pair, "py_0", ypair)
    step = 64

    def gradients(i, carry):
        rows = pl.ds(pl.multiple_of(i * step, step), step)
        total = pb[c, rows, :].astype(F32) + rp[0, 0, 0, rows, :].astype(F32)
        total += rp[1, 0, 0, rows, :].astype(F32) + pair[rows, :].astype(F32)
        qg_ref[rows, :] = (total * conv[rows, :]).astype(BF16)
        gc[rows, :] = (total * q_ref[rows, :].astype(F32)).astype(BF16)
        return carry

    for h in (0, 1):
        for n, s in enumerate((1, -1)):
            recv(rp.at[n, 0, 0, hrows(h)], f"p_{s}_0_1_{h}", zdev[-s])
        lax.fori_loop(h * half // step, (h + 1) * half // step, gradients, 0)
        if h == 0:
            send(gc.at[pl.ds(0, span)], g_rim, "rim", before)

    def corr(j, carry):
        cols = pl.ds(pl.multiple_of(j * lanes, lanes), lanes)
        grad = jnp.concatenate([gc[pl.ds(0, span), cols], gc[pl.ds(span, span), cols]], axis=1)
        grad = grad.astype(F32)
        masked = jnp.concatenate(
            [jnp.where(lane_group == g, grad, 0.0).astype(BF16) for g in range(per)], axis=0
        )
        full = dot(masked, two(x_hi, cols), NT) + dot(masked, two(x_lo, cols), NT)
        for g in range(per):
            block = full[g * span:(g + 1) * span]
            size = span
            while size > 8:
                size //= 2
                block = block[0:size] + pltpu.roll(block[size:2 * size], 2 * span - size, 1)
            sub = lax.broadcasted_iota(jnp.int32, (8, 2 * span), 0)
            for bit in (4, 2, 1):
                moved = pltpu.roll(block, 2 * span - bit, 1)
                block = jnp.where((sub // bit) % 2 == 1, moved, block)
            line = jnp.sum(block, axis=0, keepdims=True)
            taps[pl.ds(j * per + g, 1), :] = line
        return carry

    lax.fori_loop(0, tiles, corr, 0)
    tin[x] = taps[...][:, 1:span + 1]
    for d in (1, -1, 2):
        send(tin.at[x], tin.at[x], f"t_{d}", xdev[d])

    def backward(j, carry):
        cols = pl.ds(pl.multiple_of(j * lanes, lanes), lanes)
        taps_rows = pl.ds(pl.multiple_of(j * per * span, per * span), per * span)
        rimv = jnp.where(r < 15, g_rim[:, cols].astype(F32), 0.0).astype(BF16)
        lower = gc[pl.ds(0, span), cols]
        upper = gc[pl.ds(span, span), cols]
        ext = jnp.concatenate(
            [jnp.concatenate([lower, upper], axis=0), jnp.concatenate([upper, rimv], axis=0)],
            axis=1,
        )
        out = pick(dot(a_hi[taps_rows, :], ext) + dot(a_lo[taps_rows, :], ext))
        for b in range(2):
            rows = pl.ds(b * span, span)
            part = out[:, b * lanes:(b + 1) * lanes]
            kg_ref[rows, cols] = (part * v_ref[rows, cols].astype(F32)).astype(BF16)
            vg_ref[rows, cols] = (part * k_ref[rows, cols].astype(F32)).astype(BF16)
        return carry

    recv(g_rim, "rim", after)
    lax.fori_loop(0, tiles // 2, backward, 0)
    for d in (1, -1, 2):
        recv(tin.at[rowid(-d, 0, 0) // 4], f"t_{d}", xdev[-d if d != 2 else 2])
    quad = yh * 2 + core
    tin[4 + quad] = (tin[0] + tin[1]) + (tin[2] + tin[3])
    mates = ((sib, yh * 2 + 1 - core), (ytwo, 2 - 2 * yh + core), (ysib, 3 - quad))
    for n, (dev, _) in enumerate(mates):
        send(tin.at[4 + quad], tin.at[4 + quad], f"t_q{n}", dev)
    lax.fori_loop(tiles // 2, tiles, backward, 0)

    w_total(0)
    for n, (dev, place) in enumerate(mates):
        recv(tin.at[4 + place], f"t_q{n}", dev)
    total = (tin[4] + tin[5]) + (tin[6] + tin[7])
    fg_ref[...] = reversed_taps(total * (1.0 / math.sqrt(tok * 16 * group)))

    recv(yb, "x_y", ytwo)
    final = wb.at[r]
    scale = 1.0 / math.sqrt(tok * 16)

    def finish(i, carry):
        rows = pl.ds(pl.multiple_of(i * step, step), step)
        wg_ref[rows, :] = (
            (final[rows, :].astype(F32) + yb[rows, :].astype(F32)) * scale
        ).astype(BF16)
        return carry

    lax.fori_loop(0, wid // step, finish, 0)

    for copy in started:
        copy.wait_send()

    def drain(i, carry):
        desc(wb.at[0], sb.at[i], sib_base + i, sib).wait_send()
        return carry

    lax.fori_loop(0, 8, drain, 0)
    assert len(names) <= ss.shape[0], len(names)


def relay(*refs):
    ins, outs, bufs, sems = refs[0:6], refs[6:12], refs[12:18], refs[18]
    first = [pltpu.make_async_copy(a, b, sems.at[0, n]) for n, (a, b) in enumerate(zip(ins, bufs))]
    second = [pltpu.make_async_copy(a, b, sems.at[1, n]) for n, (a, b) in enumerate(zip(bufs, outs))]
    for copy in first:
        copy.start()
    for n in range(6):
        first[n].wait()
        second[n].start()
    for copy in second:
        copy.wait()


def shards(query_in, key_in, value_in, filters, out_weight, out_grad):
    tok, wid = query_in.shape
    groups, span = filters.shape
    act = jax.ShapeDtypeStruct((tok, wid), BF16)
    vmem = pl.BlockSpec(memory_space=pltpu.VMEM)
    sems = 120
    shapes = (
        act, act, act, act,
        jax.ShapeDtypeStruct((wid, wid), BF16),
        jax.ShapeDtypeStruct((groups, span), F32),
    )
    results = pl.pallas_call(
        kernel,
        out_shape=shapes,
        in_specs=[vmem] * 6,
        out_specs=[vmem] * 6,
        scratch_shapes=[
            pltpu.VMEM((span, wid), BF16),
            pltpu.VMEM((span, wid), BF16),
            pltpu.VMEM((span, wid), BF16),
            pltpu.VMEM((groups, span), F32),
            pltpu.VMEM((groups * span, 2 * span), BF16),
            pltpu.VMEM((groups * span, 2 * span), BF16),
            pltpu.VMEM((groups * span, 2 * span), BF16),
            pltpu.VMEM((groups * span, 2 * span), BF16),
            pltpu.VMEM((span + tok, wid), BF16),
            pltpu.VMEM((span + tok, wid), BF16),
            pltpu.VMEM((tok, wid), F32),
            pltpu.VMEM((tok, wid), BF16),
            pltpu.VMEM((16, wid, wid), BF16),
            pltpu.VMEM((16, tok, wid), BF16),
            pltpu.VMEM((16, tok, wid), BF16),
            pltpu.VMEM((2, 2, 4, tok, wid), BF16),
            pltpu.VMEM((3, tok, wid), BF16),
            pltpu.VMEM((tok, wid), BF16),
            pltpu.VMEM((16, wid, wid), BF16),
            pltpu.VMEM((8, wid, wid), BF16),
            pltpu.VMEM((2, 2, wid // 2, wid), BF16),
            pltpu.VMEM((2, 2, wid, wid), BF16),
            pltpu.VMEM((wid, wid), BF16),
            pltpu.VMEM((groups, 2 * span), F32),
            pltpu.VMEM((8, groups, span), F32),
            pltpu.VMEM((tok, wid), F32),
            pltpu.SemaphoreType.DMA((sems,)),
            pltpu.SemaphoreType.DMA((sems,)),
            pltpu.SemaphoreType.DMA((1,)),
        ],
        compiler_params=pltpu.CompilerParams(
            collective_id=0, has_side_effects=True, vmem_limit_bytes=67_000_000
        ),
    )(query_in, key_in, value_in, filters, out_weight, out_grad)
    anywhere = pl.BlockSpec(memory_space=pl.ANY)
    return pl.pallas_call(
        relay,
        out_shape=shapes,
        in_specs=[anywhere] * 6,
        out_specs=[anywhere] * 6,
        scratch_shapes=[pltpu.VMEM(a.shape, a.dtype) for a in shapes]
        + [pltpu.SemaphoreType.DMA((2, 6))],
    )(*results)


def solution(mesh):
    placed = (
        P("row", "col"),
        P("row", "col"),
        P("row", "col"),
        P("col", None),
        P("row", "col"),
        P("row", "col"),
    )
    return jax.shard_map(
        shards,
        mesh=mesh,
        in_specs=placed,
        out_specs=(
            P("row", "col"),
            P("row", "col"),
            P("row", "col"),
            P("row", "col"),
            P("row", "col"),
            P("col", None),
        ),
        check_vma=False,
    )
```

```python
import math

import jax
import jax.numpy as jnp
from jax import lax
from jax.experimental import pallas as pl
from jax.experimental.pallas import tpu as pltpu
from jax.sharding import PartitionSpec as P

F32 = jnp.float32
BF16 = jnp.bfloat16
MESH = pl.DeviceIdType.MESH
NT = (((1,), (1,)), ((), ()))
TN = (((0,), (0,)), ((), ()))
NN = (((1,), (0,)), ((), ()))


def dot(a, b, dims=NN):
    return lax.dot_general(a, b, dims, preferred_element_type=F32)


def split(x):
    high = x.astype(BF16)
    return high, (x - high.astype(F32)).astype(BF16)


def kernel(
    q_ref, k_ref, v_ref, f_ref, w_ref, og_ref,
    mixed_ref, qg_ref, kg_ref, vg_ref, wg_ref, fg_ref,
    k_rim, v_rim, g_rim, back,
    t_hi, t_lo, a_hi, a_lo, x_hi, x_lo, conv, gc,
    wp, gp, pb, rp, py, pair, wb, sb, xfar, xnear, yb,
    taps, tin, acc, ss, rs, ls,
):
    tok, wid = q_ref.shape
    span = f_ref.shape[1]
    groups = f_ref.shape[0]
    group = wid // groups
    lanes = 128
    tiles = wid // lanes
    per = lanes // group
    half = tok // 2
    whalf = wid // 2

    r = lax.axis_index("row")
    c = lax.axis_index("col")
    x, yh, core = r // 4, lax.rem(r // 2, 2), lax.rem(r, 2)
    yl, z = c // 8, lax.rem(c, 8)

    def rowid(dx, flip_y, flip_core):
        yy = 1 - yh if flip_y else yh
        cc = 1 - core if flip_core else core
        return lax.rem(x + dx + 4, 4) * 4 + yy * 2 + cc

    def colid(dz, flip_y):
        yy = 1 - yl if flip_y else yl
        return yy * 8 + lax.rem(z + dz + 8, 8)

    sib = (rowid(0, 0, 1), c)
    ytwo = (rowid(0, 1, 0), c)
    ysib = (rowid(0, 1, 1), c)
    xdev = {d: (rowid(d, 0, 0), c) for d in (1, -1, 2)}
    zdev = {1: (r, colid(1, 0)), -1: (r, colid(-1, 0))}
    ypair = (r, colid(0, 1))
    after = (lax.rem(r + 1, 16), c)
    before = (lax.rem(r + 15, 16), c)

    barrier = pltpu.get_barrier_semaphore()
    peers = [sib, ytwo, ysib, xdev[1], xdev[-1], xdev[2]]
    peers += [zdev[1], zdev[-1], ypair, after, before]
    for peer in peers:
        pl.semaphore_signal(barrier, inc=1, device_id=peer, device_id_type=MESH)
    pl.semaphore_wait(barrier, len(peers))

    names = {}
    started = []

    def slot(name):
        return names.setdefault(name, len(names))

    def desc(src, dst, name, dev):
        n = name if not isinstance(name, str) else slot(name)
        return pltpu.make_async_remote_copy(
            src_ref=src, dst_ref=dst, send_sem=ss.at[n], recv_sem=rs.at[n],
            device_id=dev, device_id_type=MESH,
        )

    def send(src, dst, name, dev):
        copy = desc(src, dst, name, dev)
        copy.start()
        started.append(copy)

    def recv(dst, name, dev):
        desc(dst, dst, name, dev).wait_recv()

    def add_into(dst, src):
        step = 64

        def body(i, carry):
            rows = pl.ds(pl.multiple_of(i * step, step), step)
            dst[rows, :] = (dst[rows, :].astype(F32) + src[rows, :].astype(F32)).astype(BF16)
            return carry

        lax.fori_loop(0, dst.shape[0] // step, body, 0)

    send(k_ref.at[pl.ds(tok - span, span)], k_rim, "hk", after)
    send(v_ref.at[pl.ds(tok - span, span)], v_rim, "hv", after)

    def far_half(s):
        return 0 if s == 1 else 1

    def wh(blk, h):
        return wp.at[blk, pl.ds(h * whalf, whalf)]

    for h in (0, 1):
        part = w_ref.at[pl.ds(h * whalf, whalf)]
        send(part, wh(r, h), f"w_y_{h}", ytwo)
    for k in (0, 1):
        for s in (1, -1):
            h = far_half(s) if k == 0 else 1 - far_half(s)
            part = w_ref.at[pl.ds(h * whalf, whalf)]
            send(part, wh(r, h), f"w_x{s}0_{h}", xdev[s])
    send(w_ref, wp.at[r], "w_s00", sib)
    own = pltpu.make_async_copy(w_ref, wp.at[r], ls.at[0])
    own.start()

    flip_taps = (
        lax.broadcasted_iota(jnp.int32, (span, span), 0)
        + lax.broadcasted_iota(jnp.int32, (span, span), 1)
    ) == span - 1
    flip_taps = jnp.where(flip_taps, 1.0, 0.0).astype(BF16)

    def reversed_taps(value):
        high, low = split(value)
        rest = (value - high.astype(F32) - low.astype(F32)).astype(BF16)
        return dot(high, flip_taps) + dot(low, flip_taps) + dot(rest, flip_taps)

    turn = lax.broadcasted_iota(jnp.int32, (span, span), 1)
    turn = turn - lax.broadcasted_iota(jnp.int32, (span, span), 0)

    def build(source, high_ref, low_ref, shift):
        left = turn >= shift

        def body(g, carry):
            rows = pl.ds(pl.multiple_of(g * span, span), span)
            line = jnp.broadcast_to(source[pl.ds(g, 1), :], (span, span))
            wide = pltpu.roll(line, shift, 1, stride=1, stride_axis=0)
            high = wide.astype(BF16).astype(F32)
            for ref, value in ((high_ref, high), (low_ref, wide - high)):
                ref[rows, pl.ds(0, span)] = jnp.where(left, value, 0.0).astype(BF16)
                ref[rows, pl.ds(span, span)] = jnp.where(left, 0.0, value).astype(BF16)
            return carry

        lax.fori_loop(0, groups, body, 0, unroll=2)

    lane_group = lax.broadcasted_iota(jnp.int32, (span, 2 * lanes), 1)
    lane_group = lax.rem(lane_group, lanes) // group

    def pick(full):
        mine = lane_group[:, 0:full.shape[1]]
        out = full[0:span]
        for g in range(1, per):
            out = jnp.where(mine == g, full[g * span:(g + 1) * span], out)
        return out

    def two(ref, cols):
        return jnp.concatenate(
            [ref[pl.ds(0, 2 * span), cols], ref[pl.ds(span, 2 * span), cols]], axis=1
        )

    back[...] = reversed_taps(f_ref[...])
    build(back, t_hi, t_lo, 1)
    high, low = split(k_ref[...].astype(F32) * v_ref[...].astype(F32))
    x_hi[pl.ds(span, tok), :] = high
    x_lo[pl.ds(span, tok), :] = low
    def forward(b):
        rows = pl.ds(b * span, span)
        window = pl.ds(b * span, 2 * span)

        def body(j, carry):
            cols = pl.ds(pl.multiple_of(j * lanes, lanes), lanes)
            taps_rows = pl.ds(pl.multiple_of(j * per * span, per * span), per * span)
            mh = t_hi[taps_rows, :]
            xh = x_hi[window, cols]
            full = dot(mh, xh) + dot(mh, x_lo[window, cols]) + dot(t_lo[taps_rows, :], xh)
            part = pick(full)
            conv[rows, cols] = part
            gp[c, rows, cols] = (q_ref[rows, cols].astype(F32) * part).astype(BF16)
            return carry

        lax.fori_loop(0, tiles, body, 0)

    def gh(blk, h):
        return gp.at[blk, pl.ds(h * half, half)]

    for h in (1, 0):
        if h == 0:
            recv(k_rim, "hk", before)
            recv(v_rim, "hv", before)
            rim = k_rim[...].astype(F32) * v_rim[...].astype(F32)
            high, low = split(jnp.where(r > 0, rim, 0.0))
            x_hi[pl.ds(0, span), :] = high
            x_lo[pl.ds(0, span), :] = low
        forward(h)
        for s in (1, -1):
            send(gh(c, h), gh(c, h), f"g_{s}_0_1_{h}", zdev[s])
        send(gh(c, h), gh(c, h), f"gy_0{h}", ypair)

    def g_step(flip, dist):
        for h in (1, 0):
            for s in (1, -1):
                blk = colid(-s * dist, flip)
                if dist == 4:
                    if h == far_half(s):
                        recv(gh(blk, h), f"g_{s}_{flip}_4_{h}", zdev[-s])
                    continue
                recv(gh(blk, h), f"g_{s}_{flip}_{dist}_{h}", zdev[-s])
                onward = dist < 2 if flip else dist < 3 or h == far_half(s)
                if onward:
                    send(gh(blk, h), gh(blk, h), f"g_{s}_{flip}_{dist + 1}_{h}", zdev[s])
        if not flip and dist > 2:
            for d in (-3, 3) if dist == 3 else (4,):
                blk = colid(d, 0)
                send(gp.at[blk], gp.at[blk], f"gy_{d}", ypair)

    def w_far(flip):
        for s in (1, -1):
            blk, h = rowid(-s, flip, 0), far_half(s)
            recv(wh(blk, h), f"w_x{s}{flip}_{h}", xdev[-s])
            send(wh(blk, h), wh(blk, h), f"w_far{s}{flip}", xdev[s])

    def w_near(flip):
        for s in (1, -1):
            blk, h = rowid(-s, flip, 0), 1 - far_half(s)
            recv(wh(blk, h), f"w_x{s}{flip}_{h}", xdev[-s])
            send(wp.at[blk], wp.at[blk], f"w_s{s}{flip}", sib)

    def w_two():
        blk = rowid(0, 1, 0)
        for h in (0, 1):
            recv(wh(blk, h), f"w_y_{h}", ytwo)
        for k in (0, 1):
            for s in (1, -1):
                h = far_half(s) if k == 0 else 1 - far_half(s)
                send(wh(blk, h), wh(blk, h), f"w_x{s}1_{h}", xdev[s])
        send(wp.at[blk], wp.at[blk], "w_s01", sib)

    def w_last(flip):
        blk = rowid(2, flip, 0)
        for s in (1, -1):
            h = far_half(s)
            recv(wh(blk, h), f"w_far{s}{flip}", xdev[-s])
            send(wh(blk, h), wh(blk, h), f"w_s2{flip}_{h}", sib)

    def g_partner():
        blk = colid(0, 1)
        for h in (1, 0):
            recv(gh(blk, h), f"gy_0{h}", ypair)
            for s in (1, -1):
                send(gh(blk, h), gh(blk, h), f"g_{s}_1_1_{h}", zdev[s])

    w_far(0)
    g_step(0, 1)
    w_two()
    w_near(0)
    g_step(0, 2)
    g_partner()
    w_last(0)
    build(f_ref, a_hi, a_lo, 0)
    w_far(1)
    g_step(0, 3)
    g_step(1, 1)
    w_near(1)
    g_step(0, 4)
    w_last(1)
    own.wait()
    for flip in (0, 1):
        recv(wp.at[rowid(0, flip, 1)], f"w_s0{flip}", sib)
        for d in (1, -1):
            recv(wp.at[rowid(-d, flip, 1)], f"w_s{d}{flip}", sib)
        for h in (0, 1):
            recv(wh(rowid(2, flip, 1), h), f"w_s2{flip}_{h}", sib)

    def partial(i, carry):
        dest = lax.rem(1 - yl + i // 8, 2) * 8 + lax.rem(z + i, 8)
        pb[dest] = dot(og_ref[...], wp[dest], NT).astype(BF16)
        return carry

    def hrows(h):
        return pl.ds(h * half, half)

    def p_pass(flip, dist):
        far = 3 if flip else 4
        for h in (0, 1):
            for n, s in enumerate((1, -1)):
                hh = 1 - h if s == 1 else h
                rows = hrows(hh)
                dest = colid(s * dist, flip)
                if dist == 4 and hh != far_half(s):
                    continue
                if dist < far and not (not flip and dist == 3 and hh != far_half(s)):
                    recv(rp.at[n, flip, dist, rows], f"p_{s}_{flip}_{dist + 1}_{hh}", zdev[-s])
                    add_into(pb.at[dest, rows], rp.at[n, flip, dist, rows])
                send(
                    pb.at[dest, rows], rp.at[n, flip, dist - 1, rows],
                    f"p_{s}_{flip}_{dist}_{hh}", zdev[s],
                )

    lax.fori_loop(3, 6, partial, 0)
    send(pb.at[colid(4, 1)], py, "py_4", ypair)
    p_pass(1, 3)
    lax.fori_loop(6, 16, partial, 0)
    lax.fori_loop(0, 3, partial, 0)
    g_step(1, 2)
    for d in (-3, 3, 4):
        recv(gp.at[colid(d, 1)], f"gy_{d}", ypair)

    sib_base = slot("s_0")
    for i in range(1, 8):
        slot(f"s_{i}")

    def order_row(i, cc):
        dx = jnp.where(i < 2, 2, jnp.where(i >= 6, 0, jnp.where(lax.rem(i, 2) == 0, 1, 3)))
        flip = jnp.where(i < 2, 1 - i, jnp.where(i >= 6, 7 - i, jnp.where(i < 4, 1, 0)))
        yy = lax.rem(yh + flip, 2)
        return lax.rem(x + dx, 4) * 4 + yy * 2 + cc

    def for_sib(i, carry):
        dest = order_row(i, 1 - core)
        wb[dest] = dot(gp[dest], og_ref[...], TN).astype(BF16)
        desc(wb.at[dest], sb.at[i], sib_base + i, sib).start()
        return carry

    def for_own(i, carry):
        dest = order_row(i, core)
        part = dot(gp[dest], og_ref[...], TN)
        desc(sb.at[i], sb.at[i], sib_base + i, sib).wait_recv()
        wb[dest] = (part + sb[i].astype(F32)).astype(BF16)
        return carry

    def w_half(s):
        return pl.ds(0 if s == 1 else whalf, whalf)

    def wx_far(flip):
        for n, s in enumerate((1, -1)):
            dest = rowid(2, flip, 0)
            rows = w_half(s)
            send(wb.at[dest, rows], xfar.at[n, flip], f"x_far{s}_{flip}", xdev[s])

    def wx_near(flip):
        for late in (0, 1):
            for n, s in enumerate((1, -1)):
                dest = rowid(s, flip, 0)
                h = far_half(s) if late else 1 - far_half(s)
                rows = pl.ds(h * whalf, whalf)
                if late:
                    recv(xfar.at[n, flip], f"x_far{s}_{flip}", xdev[-s])
                    add_into(wb.at[dest, rows], xfar.at[n, flip])
                send(wb.at[dest, rows], xnear.at[n, flip, rows], f"x_near{s}_{flip}_{h}", xdev[s])

    def w_total(flip):
        dest = rowid(0, flip, 0)
        for n, s in enumerate((1, -1)):
            for h in (0, 1):
                rows = pl.ds(h * whalf, whalf)
                recv(xnear.at[n, flip, rows], f"x_near{s}_{flip}_{h}", xdev[-s])
            add_into(wb.at[dest], xnear.at[n, flip])

    def mix(i, carry):
        acc[...] += dot(gp[i], wp[i])
        return carry

    lax.fori_loop(0, 4, for_sib, 0)
    lax.fori_loop(0, 2, for_own, 0)
    wx_far(1)
    recv(py, "py_4", ypair)
    add_into(pb.at[colid(4, 0)], py)
    p_pass(0, 4)
    lax.fori_loop(4, 8, for_sib, 0)
    p_pass(1, 2)
    lax.fori_loop(2, 8, for_own, 0)
    wx_near(1)
    wx_far(0)
    p_pass(0, 3)
    acc[...] = jnp.zeros_like(acc)
    lax.fori_loop(0, 5, mix, 0)
    p_pass(1, 1)
    wx_near(0)
    lax.fori_loop(5, 10, mix, 0)
    p_pass(0, 2)
    blk = colid(0, 1)
    for h in (1, 0):
        rows = hrows(h)
        for n, s in enumerate((1, -1)):
            recv(rp.at[n, 1, 0, rows], f"p_{s}_1_1_{h}", zdev[-s])
            add_into(pb.at[blk, rows], rp.at[n, 1, 0, rows])
    send(pb.at[blk], pair, "py_0", ypair)
    w_total(1)
    send(wb.at[rowid(0, 1, 0)], yb, "x_y", ytwo)
    p_pass(0, 1)
    lax.fori_loop(10, 16, mix, 0)
    mixed_ref[...] = acc[...].astype(BF16)

    recv(pair, "py_0", ypair)
    step = 64

    def gradients(i, carry):
        rows = pl.ds(pl.multiple_of(i * step, step), step)
        total = pb[c, rows, :].astype(F32) + rp[0, 0, 0, rows, :].astype(F32)
        total += rp[1, 0, 0, rows, :].astype(F32) + pair[rows, :].astype(F32)
        qg_ref[rows, :] = (total * conv[rows, :]).astype(BF16)
        gc[rows, :] = (total * q_ref[rows, :].astype(F32)).astype(BF16)
        return carry

    for h in (0, 1):
        for n, s in enumerate((1, -1)):
            recv(rp.at[n, 0, 0, hrows(h)], f"p_{s}_0_1_{h}", zdev[-s])
        lax.fori_loop(h * half // step, (h + 1) * half // step, gradients, 0)
        if h == 0:
            send(gc.at[pl.ds(0, span)], g_rim, "rim", before)

    def corr(j, carry):
        cols = pl.ds(pl.multiple_of(j * lanes, lanes), lanes)
        grad = jnp.concatenate([gc[pl.ds(0, span), cols], gc[pl.ds(span, span), cols]], axis=1)
        grad = grad.astype(F32)
        masked = jnp.concatenate(
            [jnp.where(lane_group == g, grad, 0.0).astype(BF16) for g in range(per)], axis=0
        )
        full = dot(masked, two(x_hi, cols), NT) + dot(masked, two(x_lo, cols), NT)
        for g in range(per):
            block = full[g * span:(g + 1) * span]
            size = span
            while size > 8:
                size //= 2
                block = block[0:size] + pltpu.roll(block[size:2 * size], 2 * span - size, 1)
            sub = lax.broadcasted_iota(jnp.int32, (8, 2 * span), 0)
            for bit in (4, 2, 1):
                moved = pltpu.roll(block, 2 * span - bit, 1)
                block = jnp.where((sub // bit) % 2 == 1, moved, block)
            line = jnp.sum(block, axis=0, keepdims=True)
            taps[pl.ds(j * per + g, 1), :] = line
        return carry

    lax.fori_loop(0, tiles, corr, 0)
    tin[x] = taps[...][:, 1:span + 1]
    for d in (1, -1, 2):
        send(tin.at[x], tin.at[x], f"t_{d}", xdev[d])

    def backward(j, carry):
        cols = pl.ds(pl.multiple_of(j * lanes, lanes), lanes)
        taps_rows = pl.ds(pl.multiple_of(j * per * span, per * span), per * span)
        rimv = jnp.where(r < 15, g_rim[:, cols].astype(F32), 0.0).astype(BF16)
        lower = gc[pl.ds(0, span), cols]
        upper = gc[pl.ds(span, span), cols]
        ext = jnp.concatenate(
            [jnp.concatenate([lower, upper], axis=0), jnp.concatenate([upper, rimv], axis=0)],
            axis=1,
        )
        out = pick(dot(a_hi[taps_rows, :], ext) + dot(a_lo[taps_rows, :], ext))
        for b in range(2):
            rows = pl.ds(b * span, span)
            part = out[:, b * lanes:(b + 1) * lanes]
            kg_ref[rows, cols] = (part * v_ref[rows, cols].astype(F32)).astype(BF16)
            vg_ref[rows, cols] = (part * k_ref[rows, cols].astype(F32)).astype(BF16)
        return carry

    recv(g_rim, "rim", after)
    lax.fori_loop(0, tiles // 2, backward, 0)
    for d in (1, -1, 2):
        recv(tin.at[rowid(-d, 0, 0) // 4], f"t_{d}", xdev[-d if d != 2 else 2])
    quad = yh * 2 + core
    tin[4 + quad] = (tin[0] + tin[1]) + (tin[2] + tin[3])
    mates = ((sib, yh * 2 + 1 - core), (ytwo, 2 - 2 * yh + core), (ysib, 3 - quad))
    for n, (dev, _) in enumerate(mates):
        send(tin.at[4 + quad], tin.at[4 + quad], f"t_q{n}", dev)
    lax.fori_loop(tiles // 2, tiles, backward, 0)

    w_total(0)
    for n, (dev, place) in enumerate(mates):
        recv(tin.at[4 + place], f"t_q{n}", dev)
    total = (tin[4] + tin[5]) + (tin[6] + tin[7])
    fg_ref[...] = reversed_taps(total * (1.0 / math.sqrt(tok * 16 * group)))

    recv(yb, "x_y", ytwo)
    final = wb.at[r]
    scale = 1.0 / math.sqrt(tok * 16)

    def finish(i, carry):
        rows = pl.ds(pl.multiple_of(i * step, step), step)
        wg_ref[rows, :] = (
            (final[rows, :].astype(F32) + yb[rows, :].astype(F32)) * scale
        ).astype(BF16)
        return carry

    lax.fori_loop(0, wid // step, finish, 0)

    for copy in started:
        copy.wait_send()

    def drain(i, carry):
        desc(wb.at[0], sb.at[i], sib_base + i, sib).wait_send()
        return carry

    lax.fori_loop(0, 8, drain, 0)
    assert len(names) <= ss.shape[0], len(names)


def relay(*refs):
    ins, outs, bufs, sems = refs[0:6], refs[6:12], refs[12:18], refs[18]
    first = [pltpu.make_async_copy(a, b, sems.at[0, n]) for n, (a, b) in enumerate(zip(ins, bufs))]
    second = [pltpu.make_async_copy(a, b, sems.at[1, n]) for n, (a, b) in enumerate(zip(bufs, outs))]
    for copy in first:
        copy.start()
    for n in range(6):
        first[n].wait()
        second[n].start()
    for copy in second:
        copy.wait()


def shards(query_in, key_in, value_in, filters, out_weight, out_grad):
    tok, wid = query_in.shape
    groups, span = filters.shape
    act = jax.ShapeDtypeStruct((tok, wid), BF16)
    vmem = pl.BlockSpec(memory_space=pltpu.VMEM)
    sems = 120
    shapes = (
        act, act, act, act,
        jax.ShapeDtypeStruct((wid, wid), BF16),
        jax.ShapeDtypeStruct((groups, span), F32),
    )
    results = pl.pallas_call(
        kernel,
        out_shape=shapes,
        in_specs=[vmem] * 6,
        out_specs=[vmem] * 6,
        scratch_shapes=[
            pltpu.VMEM((span, wid), BF16),
            pltpu.VMEM((span, wid), BF16),
            pltpu.VMEM((span, wid), BF16),
            pltpu.VMEM((groups, span), F32),
            pltpu.VMEM((groups * span, 2 * span), BF16),
            pltpu.VMEM((groups * span, 2 * span), BF16),
            pltpu.VMEM((groups * span, 2 * span), BF16),
            pltpu.VMEM((groups * span, 2 * span), BF16),
            pltpu.VMEM((span + tok, wid), BF16),
            pltpu.VMEM((span + tok, wid), BF16),
            pltpu.VMEM((tok, wid), F32),
            pltpu.VMEM((tok, wid), BF16),
            pltpu.VMEM((16, wid, wid), BF16),
            pltpu.VMEM((16, tok, wid), BF16),
            pltpu.VMEM((16, tok, wid), BF16),
            pltpu.VMEM((2, 2, 4, tok, wid), BF16),
            pltpu.VMEM((tok, wid), BF16),
            pltpu.VMEM((tok, wid), BF16),
            pltpu.VMEM((16, wid, wid), BF16),
            pltpu.VMEM((8, wid, wid), BF16),
            pltpu.VMEM((2, 2, wid // 2, wid), BF16),
            pltpu.VMEM((2, 2, wid, wid), BF16),
            pltpu.VMEM((wid, wid), BF16),
            pltpu.VMEM((groups, 2 * span), F32),
            pltpu.VMEM((8, groups, span), F32),
            pltpu.VMEM((tok, wid), F32),
            pltpu.SemaphoreType.DMA((sems,)),
            pltpu.SemaphoreType.DMA((sems,)),
            pltpu.SemaphoreType.DMA((1,)),
        ],
        compiler_params=pltpu.CompilerParams(
            collective_id=0, has_side_effects=True, vmem_limit_bytes=67_000_000
        ),
    )(query_in, key_in, value_in, filters, out_weight, out_grad)
    anywhere = pl.BlockSpec(memory_space=pl.ANY)
    return pl.pallas_call(
        relay,
        out_shape=shapes,
        in_specs=[anywhere] * 6,
        out_specs=[anywhere] * 6,
        scratch_shapes=[pltpu.VMEM(a.shape, a.dtype) for a in shapes]
        + [pltpu.SemaphoreType.DMA((2, 6))],
    )(*results)


def solution(mesh):
    placed = (
        P("row", "col"),
        P("row", "col"),
        P("row", "col"),
        P("col", None),
        P("row", "col"),
        P("row", "col"),
    )
    return jax.shard_map(
        shards,
        mesh=mesh,
        in_specs=placed,
        out_specs=(
            P("row", "col"),
            P("row", "col"),
            P("row", "col"),
            P("row", "col"),
            P("row", "col"),
            P("col", None),
        ),
        check_vma=False,
    )
```

```python
import math

import jax
import jax.numpy as jnp
from jax import lax
from jax.experimental import pallas as pl
from jax.experimental.pallas import tpu as pltpu
from jax.sharding import PartitionSpec as P

F32 = jnp.float32
BF16 = jnp.bfloat16
MESH = pl.DeviceIdType.MESH
NT = (((1,), (1,)), ((), ()))
TN = (((0,), (0,)), ((), ()))
NN = (((1,), (0,)), ((), ()))


def dot(a, b, dims=NN):
    return lax.dot_general(a, b, dims, preferred_element_type=F32)


def split(x):
    high = x.astype(BF16)
    return high, (x - high.astype(F32)).astype(BF16)


def kernel(
    q_in, k_in, v_in, f_ref, w_ref, og_in,
    mixed_out, qg_out, kg_out, vg_out, wg_out, fg_out,
    q_ref, k_ref, v_ref, og_ref,
    mixed_ref, qg_ref, kg_ref, vg_ref, wg_ref, fg_ref,
    k_rim, v_rim, g_rim, back,
    t_hi, t_lo, a_hi, a_lo, x_hi, x_lo, conv, gc,
    wp, gp, pb, rp, py, py3, pair, wb, sb, xfar, xnear, yb,
    taps, tin, acc, ss, rs, ls,
):
    tok, wid = q_ref.shape
    span = f_ref.shape[1]
    groups = f_ref.shape[0]
    group = wid // groups
    lanes = 128
    tiles = wid // lanes
    per = lanes // group
    half = tok // 2
    whalf = wid // 2

    r = lax.axis_index("row")
    c = lax.axis_index("col")
    x, yh, core = r // 4, lax.rem(r // 2, 2), lax.rem(r, 2)
    yl, z = c // 8, lax.rem(c, 8)

    def rowid(dx, flip_y, flip_core):
        yy = 1 - yh if flip_y else yh
        cc = 1 - core if flip_core else core
        return lax.rem(x + dx + 4, 4) * 4 + yy * 2 + cc

    def colid(dz, flip_y):
        yy = 1 - yl if flip_y else yl
        return yy * 8 + lax.rem(z + dz + 8, 8)

    sib = (rowid(0, 0, 1), c)
    ytwo = (rowid(0, 1, 0), c)
    xdev = {d: (rowid(d, 0, 0), c) for d in (1, -1)}
    zdev = {1: (r, colid(1, 0)), -1: (r, colid(-1, 0))}
    ypair = (r, colid(0, 1))
    after = (lax.rem(r + 1, 16), c)
    before = (lax.rem(r + 15, 16), c)

    barrier = pltpu.get_barrier_semaphore()
    peers = [(lax.rem(r + k, 16), c) for k in range(1, 16)]
    peers += [zdev[1], zdev[-1], ypair]
    for peer in peers:
        pl.semaphore_signal(barrier, inc=1, device_id=peer, device_id_type=MESH)

    def local(src, dst, n):
        copy = pltpu.make_async_copy(src, dst, ls.at[n])
        copy.start()
        return copy

    own = local(w_ref, wp.at[r], 0)
    k_copy = local(k_in, k_ref, 1)
    v_copy = local(v_in, v_ref, 2)
    q_copy = local(q_in, q_ref, 3)
    og_copy = local(og_in, og_ref, 4)

    names = {}
    started = []

    def slot(name):
        return names.setdefault(name, len(names))

    def desc(src, dst, name, dev):
        n = name if not isinstance(name, str) else slot(name)
        return pltpu.make_async_remote_copy(
            src_ref=src, dst_ref=dst, send_sem=ss.at[n], recv_sem=rs.at[n],
            device_id=dev, device_id_type=MESH,
        )

    def send(src, dst, name, dev):
        copy = desc(src, dst, name, dev)
        copy.start()
        started.append(copy)

    def recv(dst, name, dev):
        desc(dst, dst, name, dev).wait_recv()

    def add_into(dst, src):
        step = 64

        def body(i, carry):
            rows = pl.ds(pl.multiple_of(i * step, step), step)
            dst[rows, :] = (dst[rows, :].astype(F32) + src[rows, :].astype(F32)).astype(BF16)
            return carry

        lax.fori_loop(0, dst.shape[0] // step, body, 0)

    def far_half(s):
        return 0 if s == 1 else 1

    def wh(blk, h):
        return wp.at[blk, pl.ds(h * whalf, whalf)]

    def w_part(h):
        return w_ref.at[pl.ds(h * whalf, whalf)]

    flip_taps = (
        lax.broadcasted_iota(jnp.int32, (span, span), 0)
        + lax.broadcasted_iota(jnp.int32, (span, span), 1)
    ) == span - 1
    flip_taps = jnp.where(flip_taps, 1.0, 0.0).astype(BF16)

    def reversed_taps(value):
        high, low = split(value)
        rest = (value - high.astype(F32) - low.astype(F32)).astype(BF16)
        return dot(high, flip_taps) + dot(low, flip_taps) + dot(rest, flip_taps)

    turn = lax.broadcasted_iota(jnp.int32, (span, span), 1)
    turn = turn - lax.broadcasted_iota(jnp.int32, (span, span), 0)

    def build(source, high_ref, low_ref, shift):
        left = turn >= shift

        def body(g, carry):
            rows = pl.ds(pl.multiple_of(g * span, span), span)
            line = jnp.broadcast_to(source[pl.ds(g, 1), :], (span, span))
            wide = pltpu.roll(line, shift, 1, stride=1, stride_axis=0)
            high = wide.astype(BF16).astype(F32)
            for ref, value in ((high_ref, high), (low_ref, wide - high)):
                ref[rows, pl.ds(0, span)] = jnp.where(left, value, 0.0).astype(BF16)
                ref[rows, pl.ds(span, span)] = jnp.where(left, 0.0, value).astype(BF16)
            return carry

        lax.fori_loop(0, groups, body, 0, unroll=2)

    lane_group = lax.broadcasted_iota(jnp.int32, (span, 2 * lanes), 1)
    lane_group = lax.rem(lane_group, lanes) // group

    def pick(full):
        mine = lane_group[:, 0:full.shape[1]]
        out = full[0:span]
        for g in range(1, per):
            out = jnp.where(mine == g, full[g * span:(g + 1) * span], out)
        return out

    def two(ref, cols):
        return jnp.concatenate(
            [ref[pl.ds(0, 2 * span), cols], ref[pl.ds(span, 2 * span), cols]], axis=1
        )

    back[...] = reversed_taps(f_ref[...])
    build(back, t_hi, t_lo, 1)
    k_copy.wait()
    v_copy.wait()
    q_copy.wait()
    pl.semaphore_wait(barrier, len(peers))

    send(k_ref.at[pl.ds(tok - span, span)], k_rim, "hk", after)
    send(v_ref.at[pl.ds(tok - span, span)], v_rim, "hv", after)
    for k in (0, 1):
        for s in (1, -1):
            h = far_half(s) if k == 0 else 1 - far_half(s)
            send(w_part(h), wh(r, h), f"w_x{s}0_{h}", xdev[s])
    send(w_ref, wp.at[r], "w_s00", sib)

    high, low = split(k_ref[...].astype(F32) * v_ref[...].astype(F32))
    x_hi[pl.ds(span, tok), :] = high
    x_lo[pl.ds(span, tok), :] = low

    def forward(b):
        rows = pl.ds(b * span, span)
        window = pl.ds(b * span, 2 * span)

        def body(j, carry):
            cols = pl.ds(pl.multiple_of(j * lanes, lanes), lanes)
            taps_rows = pl.ds(pl.multiple_of(j * per * span, per * span), per * span)
            mh = t_hi[taps_rows, :]
            xh = x_hi[window, cols]
            full = dot(mh, xh) + dot(mh, x_lo[window, cols]) + dot(t_lo[taps_rows, :], xh)
            part = pick(full)
            conv[rows, cols] = part
            gp[c, rows, cols] = (q_ref[rows, cols].astype(F32) * part).astype(BF16)
            return carry

        lax.fori_loop(0, tiles, body, 0)

    def gh(blk, h):
        return gp.at[blk, pl.ds(h * half, half)]

    def g_step(flip, dist, h):
        for s in (1, -1):
            blk = colid(-s * dist, flip)
            if dist == 4 and h != far_half(s):
                continue
            recv(gh(blk, h), f"g_{s}_{flip}_{dist}_{h}", zdev[-s])
            onward = dist < 2 if flip else dist < 3 or (dist == 3 and h == far_half(s))
            if onward:
                send(gh(blk, h), gh(blk, h), f"g_{s}_{flip}_{dist + 1}_{h}", zdev[s])
            if not flip and dist > 2:
                send(gh(blk, h), gh(blk, h), f"gy_{s * dist if dist == 3 else 4}_{h}", ypair)

    def w_far(flip):
        for s in (1, -1):
            blk, h = rowid(-s, flip, 0), far_half(s)
            recv(wh(blk, h), f"w_x{s}{flip}_{h}", xdev[-s])
            send(wh(blk, h), wh(blk, h), f"w_far{s}{flip}", xdev[s])

    def w_near(flip):
        for s in (1, -1):
            blk, h = rowid(-s, flip, 0), 1 - far_half(s)
            recv(wh(blk, h), f"w_x{s}{flip}_{h}", xdev[-s])
            send(wp.at[blk], wp.at[blk], f"w_s{s}{flip}", sib)

    def w_two(h):
        blk = rowid(0, 1, 0)
        recv(wh(blk, h), f"w_y_{h}", ytwo)
        for s in (1, -1):
            send(wh(blk, h), wh(blk, h), f"w_x{s}1_{h}", xdev[s])
        if h == 1:
            send(wp.at[blk], wp.at[blk], "w_s01", sib)

    def w_last(flip):
        blk = rowid(2, flip, 0)
        for s in (1, -1):
            h = far_half(s)
            recv(wh(blk, h), f"w_far{s}{flip}", xdev[-s])
            send(wh(blk, h), wh(blk, h), f"w_s2{flip}_{h}", sib)

    def g_partner(h):
        blk = colid(0, 1)
        recv(gh(blk, h), f"gy_0{h}", ypair)
        for s in (1, -1):
            send(gh(blk, h), gh(blk, h), f"g_{s}_1_1_{h}", zdev[s])

    def g_own(h):
        forward(h)
        for s in (1, -1):
            send(gh(c, h), gh(c, h), f"g_{s}_0_1_{h}", zdev[s])

    g_own(1)
    for h in (0, 1):
        send(w_part(h), wh(r, h), f"w_y_{h}", ytwo)
    recv(k_rim, "hk", before)
    recv(v_rim, "hv", before)
    rim = k_rim[...].astype(F32) * v_rim[...].astype(F32)
    high, low = split(jnp.where(r > 0, rim, 0.0))
    x_hi[pl.ds(0, span), :] = high
    x_lo[pl.ds(0, span), :] = low
    g_own(0)
    for h in (1, 0):
        send(gh(c, h), gh(c, h), f"gy_0{h}", ypair)
    w_far(0)
    g_step(0, 1, 1)
    g_step(0, 1, 0)
    w_two(0)
    g_step(0, 2, 1)
    g_step(0, 2, 0)
    w_two(1)
    g_step(0, 3, 1)
    build(f_ref, a_hi, a_lo, 0)
    g_partner(1)
    g_step(0, 3, 0)
    g_partner(0)
    w_far(1)
    w_near(0)
    w_last(0)
    g_step(1, 1, 1)
    g_step(0, 4, 1)
    g_step(1, 1, 0)
    g_step(0, 4, 0)
    w_near(1)
    w_last(1)
    own.wait()
    og_copy.wait()
    for flip in (0, 1):
        recv(wp.at[rowid(0, flip, 1)], f"w_s0{flip}", sib)
        for d in (1, -1):
            recv(wp.at[rowid(-d, flip, 1)], f"w_s{d}{flip}", sib)
        for h in (0, 1):
            recv(wh(rowid(2, flip, 1), h), f"w_s2{flip}_{h}", sib)

    def partial(i, carry):
        dest = lax.rem(1 - yl + i // 8, 2) * 8 + lax.rem(z + i, 8)
        pb[dest] = dot(og_ref[...], wp[dest], NT).astype(BF16)
        return carry

    def hrows(h):
        return pl.ds(h * half, half)

    def p_pass(flip, dist, parts=(0, 1)):
        far = 3 if flip else 4
        for h in parts:
            for n, s in enumerate((1, -1)):
                hh = 1 - h if s == 1 else h
                rows = hrows(hh)
                dest = colid(s * dist, flip)
                if dist == 4 and hh != far_half(s):
                    continue
                if flip and dist == 3 and hh == far_half(s):
                    send(pb.at[dest, rows], py3.at[n], f"py_{s * 3}", ypair)
                    continue
                if not flip and dist == 3 and hh == far_half(s):
                    recv(py3.at[n], f"py_{s * 3}", ypair)
                    add_into(pb.at[dest, rows], py3.at[n])
                whole = flip and dist == 2 and hh == far_half(s)
                whole = whole or (not flip and dist == 3 and hh != far_half(s))
                if dist < far and not whole:
                    recv(rp.at[n, flip, dist, rows], f"p_{s}_{flip}_{dist + 1}_{hh}", zdev[-s])
                    add_into(pb.at[dest, rows], rp.at[n, flip, dist, rows])
                send(
                    pb.at[dest, rows], rp.at[n, flip, dist - 1, rows],
                    f"p_{s}_{flip}_{dist}_{hh}", zdev[s],
                )

    lax.fori_loop(2, 7, partial, 0)
    send(pb.at[colid(4, 1)], py, "py_4", ypair)
    p_pass(1, 3)
    p_pass(1, 2, (1,))
    lax.fori_loop(12, 13, partial, 0)
    for h in (1, 0):
        g_step(1, 2, h)
        for d in (-3, 3):
            recv(gh(colid(-d, 1), h), f"gy_{d}_{h}", ypair)
        recv(gh(colid(4, 1), h), f"gy_4_{h}", ypair)

    sib_base = slot("s_0")
    for i in range(1, 8):
        slot(f"s_{i}")

    def order_row(i, cc):
        dx = jnp.where(i < 2, 2, jnp.where(i >= 6, 0, jnp.where(lax.rem(i, 2) == 0, 1, 3)))
        flip = jnp.where(i < 2, 1 - i, jnp.where(i >= 6, 7 - i, jnp.where(i < 4, 1, 0)))
        yy = lax.rem(yh + flip, 2)
        return lax.rem(x + dx, 4) * 4 + yy * 2 + cc

    def for_sib(i, carry):
        dest = order_row(i, 1 - core)
        wb[dest] = dot(gp[dest], og_ref[...], TN).astype(BF16)
        desc(wb.at[dest], sb.at[i], sib_base + i, sib).start()
        return carry

    def for_own(i, carry):
        dest = order_row(i, core)
        part = dot(gp[dest], og_ref[...], TN)
        desc(sb.at[i], sb.at[i], sib_base + i, sib).wait_recv()
        wb[dest] = (part + sb[i].astype(F32)).astype(BF16)
        return carry

    def w_half(s):
        return pl.ds(0 if s == 1 else whalf, whalf)

    def wx_far(flip):
        for n, s in enumerate((1, -1)):
            dest = rowid(2, flip, 0)
            rows = w_half(s)
            send(wb.at[dest, rows], xfar.at[n, flip], f"x_far{s}_{flip}", xdev[s])

    def wx_near(flip, late):
        for n, s in enumerate((1, -1)):
            dest = rowid(s, flip, 0)
            h = far_half(s) if late else 1 - far_half(s)
            rows = pl.ds(h * whalf, whalf)
            if late:
                recv(xfar.at[n, flip], f"x_far{s}_{flip}", xdev[-s])
                add_into(wb.at[dest, rows], xfar.at[n, flip])
            send(wb.at[dest, rows], xnear.at[n, flip, rows], f"x_near{s}_{flip}_{h}", xdev[s])

    def w_total(flip):
        dest = rowid(0, flip, 0)
        for n, s in enumerate((1, -1)):
            for h in (0, 1):
                rows = pl.ds(h * whalf, whalf)
                recv(xnear.at[n, flip, rows], f"x_near{s}_{flip}_{h}", xdev[-s])
            add_into(wb.at[dest], xnear.at[n, flip])

    def mix(i, carry):
        acc[...] += dot(gp[i], wp[i])
        return carry

    lax.fori_loop(0, 8, for_sib, 0)
    lax.fori_loop(0, 2, for_own, 0)
    wx_far(1)
    recv(py, "py_4", ypair)
    add_into(pb.at[colid(4, 0)], py)
    p_pass(0, 4)
    p_pass(1, 2, (0,))
    lax.fori_loop(2, 4, for_own, 0)
    wx_near(1, 0)
    lax.fori_loop(7, 12, partial, 0)
    lax.fori_loop(13, 16, partial, 0)
    lax.fori_loop(0, 2, partial, 0)
    p_pass(0, 3)
    lax.fori_loop(4, 8, for_own, 0)
    wx_near(1, 1)
    wx_far(0)
    wx_near(0, 0)
    acc[...] = jnp.zeros_like(acc)
    lax.fori_loop(0, 4, mix, 0)
    p_pass(1, 1)
    lax.fori_loop(4, 7, mix, 0)
    p_pass(0, 2)
    blk = colid(0, 1)
    for h in (1, 0):
        rows = hrows(h)
        for n, s in enumerate((1, -1)):
            recv(rp.at[n, 1, 0, rows], f"p_{s}_1_1_{h}", zdev[-s])
            add_into(pb.at[blk, rows], rp.at[n, 1, 0, rows])
        send(pb.at[blk, rows], pair.at[rows], f"py_0_{h}", ypair)
    w_total(1)
    send(wb.at[rowid(0, 1, 0)], yb, "x_y", ytwo)
    wx_near(0, 1)
    lax.fori_loop(7, 10, mix, 0)
    p_pass(0, 1)
    lax.fori_loop(10, 16, mix, 0)
    mixed_ref[...] = acc[...].astype(BF16)
    results = [local(mixed_ref, mixed_out, 5)]

    for h in (1, 0):
        recv(pair.at[hrows(h)], f"py_0_{h}", ypair)
    step = 64

    def gradients(i, carry):
        rows = pl.ds(pl.multiple_of(i * step, step), step)
        total = pb[c, rows, :].astype(F32) + rp[0, 0, 0, rows, :].astype(F32)
        total += rp[1, 0, 0, rows, :].astype(F32) + pair[rows, :].astype(F32)
        qg_ref[rows, :] = (total * conv[rows, :]).astype(BF16)
        gc[rows, :] = (total * q_ref[rows, :].astype(F32)).astype(BF16)
        return carry

    for h in (0, 1):
        for n, s in enumerate((1, -1)):
            recv(rp.at[n, 0, 0, hrows(h)], f"p_{s}_0_1_{h}", zdev[-s])
        lax.fori_loop(h * half // step, (h + 1) * half // step, gradients, 0)
        if h == 0:
            send(gc.at[pl.ds(0, span)], g_rim, "rim", before)

    results.append(local(qg_ref, qg_out, 6))

    def corr(j, carry):
        cols = pl.ds(pl.multiple_of(j * lanes, lanes), lanes)
        grad = jnp.concatenate([gc[pl.ds(0, span), cols], gc[pl.ds(span, span), cols]], axis=1)
        grad = grad.astype(F32)
        masked = jnp.concatenate(
            [jnp.where(lane_group == g, grad, 0.0).astype(BF16) for g in range(per)], axis=0
        )
        full = dot(masked, two(x_hi, cols), NT) + dot(masked, two(x_lo, cols), NT)
        for g in range(per):
            block = full[g * span:(g + 1) * span]
            size = span
            while size > 8:
                size //= 2
                block = block[0:size] + pltpu.roll(block[size:2 * size], 2 * span - size, 1)
            sub = lax.broadcasted_iota(jnp.int32, (8, 2 * span), 0)
            for bit in (4, 2, 1):
                moved = pltpu.roll(block, 2 * span - bit, 1)
                block = jnp.where((sub // bit) % 2 == 1, moved, block)
            line = jnp.sum(block, axis=0, keepdims=True)
            taps[pl.ds(j * per + g, 1), :] = line
        return carry

    lax.fori_loop(0, tiles, corr, 0)
    tin[r] = taps[...][:, 1:span + 1]
    for k in (10, 6, 14, 2, 11, 5, 9, 7, 8, 15, 3, 13, 4, 12, 1):
        send(tin.at[r], tin.at[r], f"t_{k}", (lax.rem(r + k, 16), c))

    def backward(j, carry):
        cols = pl.ds(pl.multiple_of(j * lanes, lanes), lanes)
        taps_rows = pl.ds(pl.multiple_of(j * per * span, per * span), per * span)
        rimv = jnp.where(r < 15, g_rim[:, cols].astype(F32), 0.0).astype(BF16)
        lower = gc[pl.ds(0, span), cols]
        upper = gc[pl.ds(span, span), cols]
        ext = jnp.concatenate(
            [jnp.concatenate([lower, upper], axis=0), jnp.concatenate([upper, rimv], axis=0)],
            axis=1,
        )
        out = pick(dot(a_hi[taps_rows, :], ext) + dot(a_lo[taps_rows, :], ext))
        for b in range(2):
            rows = pl.ds(b * span, span)
            part = out[:, b * lanes:(b + 1) * lanes]
            kg_ref[rows, cols] = (part * v_ref[rows, cols].astype(F32)).astype(BF16)
            vg_ref[rows, cols] = (part * k_ref[rows, cols].astype(F32)).astype(BF16)
        return carry

    recv(g_rim, "rim", after)
    lax.fori_loop(0, tiles, backward, 0)
    results.append(local(kg_ref, kg_out, 7))
    results.append(local(vg_ref, vg_out, 8))
    w_total(0)
    recv(yb, "x_y", ytwo)
    final = wb.at[r]
    scale = 1.0 / math.sqrt(tok * 16)

    def finish(i, carry):
        rows = pl.ds(pl.multiple_of(i * step, step), step)
        wg_ref[rows, :] = (
            (final[rows, :].astype(F32) + yb[rows, :].astype(F32)) * scale
        ).astype(BF16)
        return carry

    lax.fori_loop(0, wid // step, finish, 0)
    results.append(local(wg_ref, wg_out, 9))
    for copy in started:
        copy.wait_send()

    def drain(i, carry):
        desc(wb.at[0], sb.at[i], sib_base + i, sib).wait_send()
        return carry

    lax.fori_loop(0, 8, drain, 0)
    for k in range(1, 16):
        recv(tin.at[lax.rem(r + 16 - k, 16)], f"t_{k}", (lax.rem(r + 16 - k, 16), c))
    total = tin[0]
    for k in range(1, 16):
        total += tin[k]
    fg_ref[...] = reversed_taps(total * (1.0 / math.sqrt(tok * 16 * group)))

    results.append(local(fg_ref, fg_out, 10))
    for copy in results:
        copy.wait()
    assert len(names) <= ss.shape[0], len(names)


def relay(*refs):
    ins, outs, bufs, sems = refs[0:6], refs[6:12], refs[12:18], refs[18]
    first = [pltpu.make_async_copy(a, b, sems.at[0, n]) for n, (a, b) in enumerate(zip(ins, bufs))]
    second = [pltpu.make_async_copy(a, b, sems.at[1, n]) for n, (a, b) in enumerate(zip(bufs, outs))]
    for copy in first:
        copy.start()
    for n in range(6):
        first[n].wait()
        second[n].start()
    for copy in second:
        copy.wait()


def shards(query_in, key_in, value_in, filters, out_weight, out_grad):
    tok, wid = query_in.shape
    groups, span = filters.shape
    act = jax.ShapeDtypeStruct((tok, wid), BF16)
    vmem = pl.BlockSpec(memory_space=pltpu.VMEM)
    anywhere = pl.BlockSpec(memory_space=pl.ANY)
    sems = 144
    shapes = (
        act, act, act, act,
        jax.ShapeDtypeStruct((wid, wid), BF16),
        jax.ShapeDtypeStruct((groups, span), F32),
    )
    results = pl.pallas_call(
        kernel,
        out_shape=shapes,
        in_specs=[anywhere] * 3 + [vmem] + [anywhere] * 2,
        out_specs=[anywhere] * 6,
        scratch_shapes=[pltpu.VMEM((tok, wid), BF16)] * 4
        + [pltpu.VMEM(a.shape, a.dtype) for a in shapes]
        + [
            pltpu.VMEM((span, wid), BF16),
            pltpu.VMEM((span, wid), BF16),
            pltpu.VMEM((span, wid), BF16),
            pltpu.VMEM((groups, span), F32),
            pltpu.VMEM((groups * span, 2 * span), BF16),
            pltpu.VMEM((groups * span, 2 * span), BF16),
            pltpu.VMEM((groups * span, 2 * span), BF16),
            pltpu.VMEM((groups * span, 2 * span), BF16),
            pltpu.VMEM((span + tok, wid), BF16),
            pltpu.VMEM((span + tok, wid), BF16),
            pltpu.VMEM((tok, wid), F32),
            pltpu.VMEM((tok, wid), BF16),
            pltpu.VMEM((16, wid, wid), BF16),
            pltpu.VMEM((16, tok, wid), BF16),
            pltpu.VMEM((16, tok, wid), BF16),
            pltpu.VMEM((2, 2, 4, tok, wid), BF16),
            pltpu.VMEM((tok, wid), BF16),
            pltpu.VMEM((2, tok // 2, wid), BF16),
            pltpu.VMEM((tok, wid), BF16),
            pltpu.VMEM((16, wid, wid), BF16),
            pltpu.VMEM((8, wid, wid), BF16),
            pltpu.VMEM((2, 2, wid // 2, wid), BF16),
            pltpu.VMEM((2, 2, wid, wid), BF16),
            pltpu.VMEM((wid, wid), BF16),
            pltpu.VMEM((groups, 2 * span), F32),
            pltpu.VMEM((16, groups, span), F32),
            pltpu.VMEM((tok, wid), F32),
            pltpu.SemaphoreType.DMA((sems,)),
            pltpu.SemaphoreType.DMA((sems,)),
            pltpu.SemaphoreType.DMA((11,)),
        ],
        compiler_params=pltpu.CompilerParams(
            collective_id=0, has_side_effects=True, vmem_limit_bytes=67_000_000
        ),
    )(query_in, key_in, value_in, filters, out_weight, out_grad)
    return pl.pallas_call(
        relay,
        out_shape=shapes,
        in_specs=[anywhere] * 6,
        out_specs=[anywhere] * 6,
        scratch_shapes=[pltpu.VMEM(a.shape, a.dtype) for a in shapes]
        + [pltpu.SemaphoreType.DMA((2, 6))],
    )(*results)


def solution(mesh):
    placed = (
        P("row", "col"),
        P("row", "col"),
        P("row", "col"),
        P("col", None),
        P("row", "col"),
        P("row", "col"),
    )
    return jax.shard_map(
        shards,
        mesh=mesh,
        in_specs=placed,
        out_specs=(
            P("row", "col"),
            P("row", "col"),
            P("row", "col"),
            P("row", "col"),
            P("row", "col"),
            P("col", None),
        ),
        check_vma=False,
    )
```
